32 devices in a mesh: role: 2 (over core), grp: 4 (over y, x), dev: 4 (over z).
Axes of the slice: x: 2, y: 2, z: 4, core: 2. Of those that a mesh axis runs over, the one named last changes fastest.
Arguments:
- tokens: bfloat16 [768, 2048], P(('role', 'grp', 'dev')), may hold values from -6 to 6
- norm_gain: float32 [2048], replicated, may hold values from 0.1 to 1.9
- q_gain: float32 [128], replicated, may hold values from 0.1 to 1.9
- k_gain: float32 [128], replicated, may hold values from 0.1 to 1.9
- post_gain: float32 [2048], replicated, may hold values from 0.1 to 1.9
- w_query: bfloat16 [2048, 4096], P(None, 'dev'), may hold values from -0.125 to 0.125
- w_keyvalue: bfloat16 [2048, 1024], P(None, 'dev'), may hold values from -0.125 to 0.125
- w_out: bfloat16 [4096, 2048], P('dev'), may hold values from -0.09375 to 0.09375
- cache_keys: bfloat16 [768, 4, 128, 128], P(('role', 'grp', 'dev')), may hold values from -400 to 400
- cache_values: bfloat16 [768, 4, 128, 128], P(('role', 'grp', 'dev')), may hold values from -6 to 6
- lengths: int32 [768], P(('role', 'grp', 'dev')), may hold values from 1 to 128
- expert_ids: int32 [768, 8], P(('role', 'grp', 'dev')), may hold values from 0 to 15, all different within a row; in each aligned block of 24 rows (0 to 23, 24 to 47, ...) at most 13 rows name the same one
- w_gate: bfloat16 [16, 2048, 768], P(('grp', 'dev'), None, 'role'), may hold values from -0.125 to 0.125
- w_up: bfloat16 [16, 2048, 768], P(('grp', 'dev'), None, 'role'), may hold values from -0.125 to 0.125
- w_down: bfloat16 [16, 768, 2048], P(('grp', 'dev'), 'role'), may hold values from -0.21875 to 0.21875
Outputs:
- layer_out: bfloat16 [768, 2048], P(('role', 'grp', 'dev'))
The draws below stay inside these ranges and needn't reach their ends.
Inputs may be any that keep to these rules, and one draw needn't show every extreme that they name: `expert_ids`: each row names 8 different experts. Among the 24 rows of one device no expert is named more than 13 times; in the rows of some devices one expert is named exactly 13 times.
All inputs are finite; a program needn't handle non-finite values.
Results may differ from the reference program's by a relative error of at most 0.0099.
Values may be sent and summed in bfloat16 or wider, within the bound.
No kernel may reach another device: no remote copies, remote signals or barrier semaphores. Data moves between devices by JAX's collectives and lax.ppermute only.
A program may use at most 128 MiB of HBM per device.

```python
import math
import jax
import jax.numpy as jnp
import numpy as np
from jax import lax

D = 2048
Q_HEADS = 32
KV_HEADS = 4
HD = 128
FF_E = 768
TOPK = 8
CACHE = 128
REQ_DEV = 24
EXPERTS = 16
REQUESTS = 768
CAP = 13


def draw_cache_keys(key, part):
    dims_shape = (REQUESTS, KV_HEADS, CACHE, HD)
    values = jnp.clip(jax.random.normal(key, dims_shape, jnp.float32), -6.0, 6.0)
    return values.astype(jnp.bfloat16)


def touch_ends(values, rng, least, top_value):
    longest = values.shape.index(max(values.shape))
    spots = []
    for shift in (0, 1):
        where = [jax.random.randint(jax.random.fold_in(rng, axis), (), 0, length) for axis, length in enumerate(values.shape)]
        where[longest] = (where[longest] + shift) % values.shape[longest]
        spots.append(tuple(where))
    return values.at[spots[0]].set(least).at[spots[1]].set(top_value)


def levels(key, dims, shards, low, high):
    level = 1.0
    for axis_at, parts in shards:
        draws = jax.random.uniform(jax.random.fold_in(jax.random.fold_in(key, 6), axis_at), (parts,), jnp.float32, low / len(shards), high / len(shards))
        level = level * jnp.repeat(jnp.exp(draws), dims[axis_at] // parts).reshape((-1,) + (1,) * (len(dims) - 1 - axis_at))
    return level


def routed_block(key, own, number, rows, number_of, top, limit, lean):
    sequence = jax.random.permutation(key, number_of)
    crowded, usual = shares(number_of, rows * top, limit, lean, True), shares(number_of, rows * top, limit, lean, False)
    places = jnp.arange(number_of)

    def named(tallies, turn):
        used = int((tallies > 0).sum())
        fixed = max(1, used // 4)
        shifted = fixed + (places - fixed + turn * (used - fixed)) % max(1, number_of - fixed)
        return jnp.zeros((number_of,), jnp.int32).at[sequence[jnp.where(places < fixed, places, shifted)]].set(jnp.asarray(tallies, jnp.int32))

    tallies = jnp.where(number % 4 == 0, named(crowded, number // 4), named(usual, number - number // 4 - 1))
    mixed = jax.random.permutation(jax.random.fold_in(own, 3), number_of)
    donor, taker = mixed[0:number_of // 2 * 2:2], mixed[1:number_of // 2 * 2:2]
    room = jnp.minimum(tallies[donor] - 1, limit - tallies[taker]) // 2
    room = jnp.where((donor == sequence[0]) | (taker == sequence[0]) | (tallies[taker] == 0), 0, jnp.maximum(room, 0))
    shifted = jax.random.randint(jax.random.fold_in(own, 4), (number_of // 2,), 0, 1 << 20) % (room + 1)
    tallies = tallies.at[donor].add(-shifted).at[taker].add(shifted)
    items = jnp.searchsorted(jnp.cumsum(tallies), jnp.arange(rows * top), side="right").astype(jnp.int32)
    listing = items.reshape(top, rows).T
    listing = listing[jax.random.permutation(jax.random.fold_in(own, 1), rows)]
    turn = jax.random.randint(jax.random.fold_in(own, 2), (rows, 1), 0, top)
    return jnp.take_along_axis(listing, (jnp.arange(top)[None, :] + turn) % top, axis=1)


def shares(count, total, most, lean, full):
    weights = [(1 << 20) // math.isqrt(standing ** lean) + 1 for standing in range(1, count + 1)]
    largest = most if full else min(most, max(-(-total // count), total * weights[0] // sum(weights)))
    least = 1 if total - largest >= count - 1 else 0
    counts, surplus = [largest] + [least] * (count - 1), total - largest - least * (count - 1)
    while surplus > 0:
        movable = [i for i in range(1, count) if counts[i] < largest] or [i for i in range(1, count) if counts[i] < most]
        pool, budget = sum([weights[i] for i in movable]), surplus
        for i in movable:
            extra = min(most - counts[i], max(1, budget * weights[i] // pool), surplus)
            counts[i] = counts[i] + extra
            surplus = surplus - extra
    return np.array(counts)


def gaussian(own_key, dims, deviation, limit, split=(), held_as=jnp.bfloat16):
    entries = jax.random.normal(own_key, dims, jnp.float32) * deviation
    if len(split) > 0:
        entries = levels(own_key, dims, split, -0.22, 0.18) * entries
    return jnp.clip(entries, min=-limit, max=limit).astype(held_as)


def setup_inputs(seed: int = 0) -> dict:
    streams_of = jax.random.split(jax.random.key(seed), 16)
    tokens = gaussian(streams_of[0], (REQUESTS, D), 1.0, 6.0, ((0, 32),))
    norm_gain = jnp.clip(1.0 + 0.18 * jax.random.normal(streams_of[1], (D,), jnp.float32), 0.1, 1.9)
    q_gain = jnp.clip(1.0 + 0.18 * jax.random.normal(streams_of[2], (HD,), jnp.float32), 0.1, 1.9)
    k_gain = jnp.clip(1.0 + 0.18 * jax.random.normal(streams_of[3], (HD,), jnp.float32), 0.1, 1.9)
    post_gain = jnp.clip(1.0 + 0.18 * jax.random.normal(streams_of[4], (D,), jnp.float32), 0.1, 1.9)
    w_query = gaussian(streams_of[5], (D, Q_HEADS * HD), D ** -0.5, 0.125, ((1, 4),))
    w_keyvalue = gaussian(streams_of[6], (D, 2 * KV_HEADS * HD), D ** -0.5, 0.125, ((1, 4),))
    w_out = gaussian(streams_of[7], (Q_HEADS * HD, D), (Q_HEADS * HD) ** -0.5, 0.09375, ((0, 4),))
    cache_keys = draw_cache_keys(jax.random.fold_in(streams_of[15], 71), 0)
    cache_values = gaussian(streams_of[9], (REQUESTS, KV_HEADS, CACHE, HD), 1.0, 6.0, ((0, 32),))
    lengths = touch_ends(jax.random.randint(streams_of[10], (REQUESTS,), 1, CACHE + 1), jax.random.fold_in(streams_of[10], 1), 1, CACHE).astype(jnp.int32)
    expert_ids_keys = jax.random.split(jax.random.fold_in(streams_of[11], 1), REQUESTS // REQ_DEV)
    expert_ids_turns = jax.random.permutation(jax.random.fold_in(streams_of[11], 3), REQUESTS // REQ_DEV)
    expert_ids = jax.vmap(lambda own, number: routed_block(jax.random.fold_in(streams_of[11], 2), own, number, REQ_DEV, EXPERTS, TOPK, CAP, 2))(expert_ids_keys, expert_ids_turns).reshape((REQUESTS, TOPK))
    w_gate = gaussian(streams_of[12], (EXPERTS, D, FF_E), D ** -0.5, 0.125, ((0, 16), (2, 2)))
    w_up = gaussian(streams_of[13], (EXPERTS, D, FF_E), D ** -0.5, 0.125, ((0, 16), (2, 2)))
    w_down = gaussian(streams_of[14], (EXPERTS, FF_E, D), FF_E ** -0.5, 0.21875, ((0, 16), (1, 2)))
    return dict(tokens=tokens, norm_gain=norm_gain, q_gain=q_gain, k_gain=k_gain, post_gain=post_gain, w_query=w_query, w_keyvalue=w_keyvalue, w_out=w_out, cache_keys=cache_keys, cache_values=cache_values, lengths=lengths, expert_ids=expert_ids, w_gate=w_gate, w_up=w_up, w_down=w_down)


epsilon = 1e-06
rope_base = 1000000.0

def rms_scale(values, gain):
    widened = values.astype(jnp.float32)
    mean_square = lax.optimization_barrier(jnp.mean(widened * widened, axis=-1, keepdims=True))
    return widened * lax.rsqrt(mean_square + epsilon) * gain.astype(jnp.float32)

def rotate(values, positions):
    half_dim = values.shape[-1] // 2
    frequency = rope_base ** (-jnp.arange(half_dim, dtype=jnp.float32) / half_dim)
    angles = positions.astype(jnp.float32)[:, None, None] * frequency[None, None, :]
    cosine = jnp.cos(angles)
    sine_part = jnp.sin(angles)
    first_half = values[..., :half_dim]
    second_half = values[..., half_dim:]
    return jnp.concatenate([first_half * cosine - second_half * sine_part, second_half * cosine + first_half * sine_part], axis=-1)

def attend(queries, fresh_kv, cache_keys, cache_values, lengths, q_gain, k_gain):
    batch_rows = queries.shape[0]
    kv_heads = cache_keys.shape[1]
    cache_len = cache_keys.shape[2]
    head_dim = cache_keys.shape[3]
    head_count = queries.shape[1] // head_dim
    group_size = head_count // kv_heads
    scaled_q = rotate(rms_scale(queries.reshape(batch_rows, head_count, head_dim), q_gain), lengths).astype(jnp.bfloat16)
    fresh_keys = fresh_kv[:, :kv_heads * head_dim].reshape(batch_rows, kv_heads, head_dim)
    fresh_values = fresh_kv[:, kv_heads * head_dim:].reshape(batch_rows, kv_heads, head_dim)
    scaled_k = rotate(rms_scale(fresh_keys, k_gain), lengths).astype(jnp.bfloat16)
    grouped = scaled_q.reshape(batch_rows, kv_heads, group_size, head_dim).astype(jnp.float32)
    factor = head_dim ** (-0.5)
    old_scores = jnp.einsum('rgqd,rgkd->rgqk', grouped, cache_keys.astype(jnp.float32)) * factor
    new_scores = jnp.einsum('rgqd,rgd->rgq', grouped, scaled_k.astype(jnp.float32)) * factor
    visible = jnp.arange(cache_len, dtype=jnp.int32)[None, :] < lengths[:, None]
    old_scores = jnp.where(visible[:, None, None, :], old_scores, -jnp.inf)
    highest = jnp.maximum(lax.optimization_barrier(jnp.max(old_scores, axis=-1)), new_scores)
    old_weights = jnp.exp(old_scores - highest[..., None])
    new_weights = jnp.exp(new_scores - highest)
    denominator = lax.optimization_barrier(jnp.sum(old_weights, axis=-1)) + new_weights
    old_weights = (old_weights / denominator[..., None]).astype(jnp.bfloat16)
    new_weights = (new_weights / denominator).astype(jnp.bfloat16)
    mixture = jnp.einsum('rgqk,rgkd->rgqd', old_weights.astype(jnp.float32), cache_values.astype(jnp.float32))
    mixture = mixture + new_weights.astype(jnp.float32)[..., None] * fresh_values.astype(jnp.float32)[:, :, None, :]
    return mixture.reshape(batch_rows, head_count * head_dim).astype(jnp.bfloat16)

def reference(tokens, norm_gain, q_gain, k_gain, post_gain, w_query, w_keyvalue, w_out, cache_keys, cache_values, lengths, expert_ids, w_gate, w_up, w_down):
    normed = rms_scale(tokens, norm_gain).astype(jnp.bfloat16)
    queries = jnp.dot(normed, w_query, preferred_element_type=jnp.float32).astype(jnp.bfloat16)
    fresh_kv = jnp.dot(normed, w_keyvalue, preferred_element_type=jnp.float32).astype(jnp.bfloat16)
    blocks = REQUESTS // REQ_DEV

    def per_block(pieces):
        return attend(pieces[0], pieces[1], pieces[2], pieces[3], pieces[4], q_gain, k_gain)
    mixture = lax.map(per_block, (queries.reshape(blocks, REQ_DEV, Q_HEADS * HD), fresh_kv.reshape(blocks, REQ_DEV, 2 * KV_HEADS * HD), cache_keys.reshape(blocks, REQ_DEV, KV_HEADS, CACHE, HD), cache_values.reshape(blocks, REQ_DEV, KV_HEADS, CACHE, HD), lengths.reshape(blocks, REQ_DEV)))
    mixture = mixture.reshape(REQUESTS, Q_HEADS * HD)
    hidden = tokens.astype(jnp.float32) + jnp.dot(mixture, w_out, preferred_element_type=jnp.float32)
    ready = rms_scale(hidden, post_gain).astype(jnp.bfloat16)
    bound = min(REQUESTS, blocks * CAP)
    padded = jnp.concatenate([ready, jnp.zeros((1, D), jnp.bfloat16)], axis=0)

    def per_expert(carry, inputs):
        index, gate_w, up_w, down_w = inputs
        chosen = lax.optimization_barrier(jnp.sum((expert_ids == index).astype(jnp.int32), axis=1)) > 0
        picked_rows = jnp.nonzero(chosen, size=bound, fill_value=REQUESTS)[0].astype(jnp.int32)
        gathered = padded[picked_rows]
        gate_part = jnp.dot(gathered, gate_w, preferred_element_type=jnp.float32)
        upper_part = jnp.dot(gathered, up_w, preferred_element_type=jnp.float32)
        activated = (jax.nn.silu(gate_part) * upper_part).astype(jnp.bfloat16)
        result = jnp.dot(activated, down_w, preferred_element_type=jnp.float32).astype(jnp.bfloat16)
        return (carry.at[picked_rows].add(result.astype(jnp.float32)), None)
    summed, unused = lax.scan(per_expert, jnp.zeros((REQUESTS + 1, D), jnp.float32), (jnp.arange(EXPERTS, dtype=jnp.int32), w_gate, w_up, w_down))
    output = hidden + summed[:REQUESTS] / TOPK
    return output.astype(jnp.bfloat16)
```

```python
import functools

import jax
import jax.numpy as jnp
from jax import lax
from jax.experimental import pallas as pl
from jax.experimental.pallas import tpu as pltpu
from jax.sharding import PartitionSpec as P

epsilon = 1e-06
rope_base = 1000000.0
LANES = 128
VMEM = pl.BlockSpec(memory_space=pltpu.VMEM)
SMEM = pl.BlockSpec(memory_space=pltpu.SMEM)
F32 = jnp.float32
BF16 = jnp.bfloat16


def call(kernel, outs, specs, args, scratch=(), cost=None, limit=None):
    flops, moved = cost or (0, 0)
    return pl.pallas_call(
        kernel,
        out_shape=[jax.ShapeDtypeStruct(shape, dtype) for shape, dtype in outs],
        in_specs=list(specs),
        out_specs=[VMEM] * len(outs),
        scratch_shapes=list(scratch),
        cost_estimate=pl.CostEstimate(flops=flops, bytes_accessed=moved, transcendentals=0),
        compiler_params=pltpu.CompilerParams(vmem_limit_bytes=limit),
    )(*args)


def exchange(pieces, axis, size):
    got = [pieces[0]]
    for step in range(1, size):
        got.append(lax.ppermute(pieces[step], axis, [(i, i ^ step) for i in range(size)]))
    return got


def rms(values, gain):
    mean_square = jnp.mean(values * values, axis=-1, keepdims=True)
    return values * lax.rsqrt(mean_square + epsilon) * gain


def stack(refs):
    return jnp.concatenate([ref[...].astype(F32) for ref in refs], axis=0)


def project_kernel(count, *refs):
    blocks, (gain, w_query, w_keyvalue, ids), outs = refs[:count], refs[count : count + 4], refs[count + 4 :]
    rows = blocks[0].shape[0]
    query_width = w_query.shape[1]
    kv_width = w_keyvalue.shape[1]
    normed = rms(stack(blocks), gain[...]).astype(BF16)
    queries = jnp.dot(normed, w_query[...], preferred_element_type=F32)
    fresh = jnp.dot(normed, w_keyvalue[...], preferred_element_type=F32)
    for step in range(count):
        own = slice(step * rows, (step + 1) * rows)
        outs[step][:, :query_width] = queries[own].astype(BF16)
        outs[step][:, query_width : query_width + kv_width] = fresh[own].astype(BF16)
        outs[step][:, query_width + kv_width :] = ids[...]


def attend_kernel(count, me_ref, *refs):
    messages = refs[:count]
    q_gain, k_gain, cosine, sine, bias, cache_keys, cache_values = refs[count : count + 7]
    outs = refs[count + 7 : 2 * count + 7]
    q_rot, k_rot, v_new, kv_all, mixed = refs[2 * count + 7 :]
    me = me_ref[0]
    rows, heads, places, dim = cache_keys.shape
    group = q_rot.shape[1] // rows
    query_width = group * dim
    kv_width = kv_all.shape[2]
    cos, sin = cosine[...], sine[...]

    def turn(values, gain):
        values = rms(values, gain)
        return values * cos + pltpu.roll(values, dim // 2, 1) * sin

    for step in range(count):
        kv_all[me ^ step] = messages[step][:, query_width : query_width + kv_width].astype(F32)
        for h in range(group):
            piece = messages[step][:, h * dim : (h + 1) * dim].astype(F32)
            q_rot[step, pl.ds(h, rows, stride=group), :] = turn(piece, q_gain[...])
    for h in range(2 * heads):
        column = h * dim
        piece = kv_all[column // kv_width, :, column % kv_width : column % kv_width + dim]
        if h < heads:
            k_rot[h] = turn(piece, k_gain[...]).astype(BF16).astype(F32)
        else:
            v_new[h - heads] = piece
    factor = dim ** (-0.5)
    seen = bias[...][:, None, :]
    for step in range(count):
        head = me ^ step
        query = q_rot[step].reshape(rows, group, dim).astype(BF16)
        old = (
            jnp.einsum("rqd,rkd->rqk", query, cache_keys[:, head], preferred_element_type=F32) * factor
            + seen
        )
        new = jnp.sum(query.astype(F32) * k_rot[head][:, None, :], axis=-1, keepdims=True) * factor
        highest = jnp.maximum(jnp.max(old, axis=-1, keepdims=True), new)
        old = jnp.exp(old - highest)
        new = jnp.exp(new - highest)
        total = jnp.sum(old, axis=-1, keepdims=True) + new
        old = (old / total).astype(BF16)
        new = (new / total).astype(BF16).astype(F32)
        out = jnp.einsum("rqk,rkd->rqd", old, cache_values[:, head], preferred_element_type=F32)
        out = out + new * v_new[head][:, None, :]
        mixed[...] = out.reshape(rows * group, dim)
        for h in range(group):
            outs[step][:, h * dim : (h + 1) * dim] = mixed[pl.ds(h, rows, stride=group), :].astype(BF16)


def out_kernel(count, *refs):
    blocks, w_out, outs = refs[:count], refs[count], refs[count + 1 :]
    rows = blocks[0].shape[0]
    partial = jnp.dot(stack(blocks).astype(BF16), w_out[...], preferred_element_type=F32)
    for step in range(count):
        outs[step][...] = partial[step * rows : (step + 1) * rows].astype(outs[step].dtype)


def ready_kernel(count, *refs):
    blocks, (tokens, gain), (hidden, ready) = refs[:count], refs[count : count + 2], refs[count + 2 :]
    total = blocks[0][...]
    for block in blocks[1:]:
        total = total + block[...].astype(F32)
    total = tokens[...].astype(F32) + total
    hidden[...] = total
    ready[...] = rms(total, gain[...]).astype(BF16)


def route_kernel(count, groups, capacity, stride, where_ref, *refs):
    ids, out = refs[:count], refs[count]
    dev, grp = where_ref[0], where_ref[1]
    table = stack(ids)
    total = table.shape[0]
    rows = total // count
    lane = lax.broadcasted_iota(jnp.int32, (total, LANES), 1)
    named = jnp.zeros((total, LANES), F32)
    for step in range(groups):
        expert = ((grp ^ step) * count + dev).astype(F32)
        hit = jnp.max(jnp.where(table == expert, 1.0, 0.0), axis=1, keepdims=True)
        named = jnp.where(lane == step, hit, named)
    down = lax.broadcasted_iota(jnp.int32, (total, total), 0)
    across = lax.broadcasted_iota(jnp.int32, (total, total), 1)
    earlier = jnp.where((across < down) & (across // rows == down // rows), 1.0, 0.0)
    rank = jnp.dot(earlier.astype(BF16), named.astype(BF16), preferred_element_type=F32)
    source = (lax.broadcasted_iota(jnp.int32, (total, LANES), 0) // rows).astype(F32)
    slot = rank + source * capacity + lane.astype(F32) * stride
    place = lax.broadcasted_iota(jnp.int32, (total, groups * stride), 1).astype(F32)
    chosen = jnp.zeros((total, groups * stride), F32)
    for step in range(groups):
        match = (place == slot[:, step : step + 1]) & (named[:, step : step + 1] > 0)
        chosen = jnp.where(match, 1.0, chosen)
    out[...] = chosen.astype(BF16)


def pack_kernel(count, *refs):
    blocks, choice, outs = refs[:count], refs[count], refs[count + 1 :]
    stride = outs[0].shape[0]
    packed = lax.dot_general(
        choice[...], stack(blocks).astype(BF16), (((0,), (0,)), ((), ())), preferred_element_type=F32
    )
    for step, out in enumerate(outs):
        out[...] = packed[step * stride : (step + 1) * stride].astype(BF16)


def expert_kernel(groups, *refs):
    blocks, weights, outs = refs[:groups], refs[groups : groups + 6], refs[groups + 6 :]
    stride = outs[0].shape[0]
    inputs = stack(blocks).astype(BF16)
    total = None
    for half in range(2):
        gate, up, down = weights[3 * half : 3 * half + 3]
        gated = jnp.dot(inputs, gate[...], preferred_element_type=F32)
        upper = jnp.dot(inputs, up[...], preferred_element_type=F32)
        active = (gated / (1.0 + jnp.exp(-gated)) * upper).astype(BF16)
        part = jnp.dot(active, down[...], preferred_element_type=F32)
        total = part if total is None else total + part
    for step, out in enumerate(outs):
        out[...] = total[step * stride : (step + 1) * stride].astype(BF16)


def combine_kernel(groups, *refs):
    blocks, choice, outs = refs[:groups], refs[groups], refs[groups + 1 :]
    summed = jnp.dot(choice[...], stack(blocks).astype(BF16), preferred_element_type=F32)
    rows = outs[0].shape[0]
    for step, out in enumerate(outs):
        out[...] = summed[step * rows : (step + 1) * rows].astype(out.dtype)


def final_kernel(count, picks, *refs):
    blocks, hidden, out = refs[:count], refs[count], refs[count + 1]
    total = blocks[0][...]
    for block in blocks[1:]:
        total = total + block[...].astype(F32)
    out[...] = (hidden[...] + total / picks).astype(BF16)


def body(
    tokens,
    norm_gain,
    q_gain,
    k_gain,
    post_gain,
    w_query,
    w_keyvalue,
    w_out,
    cache_keys,
    cache_values,
    lengths,
    expert_ids,
    w_gate,
    w_up,
    w_down,
):
    count, groups = lax.axis_size("dev"), lax.axis_size("grp")
    rows, width = tokens.shape
    picks = expert_ids.shape[1]
    heads, places, dim = cache_keys.shape[1:]
    query_width, kv_width = w_query.shape[1], w_keyvalue.shape[1]
    group = query_width // dim
    experts = count * groups
    capacity = min(rows, max(3, (rows * picks + experts - 1) // experts + 1))
    stride = -(-count * capacity // 8) * 8
    dev, grp = lax.axis_index("dev"), lax.axis_index("grp")

    swap = [(0, 1), (1, 0)]
    own_weights = [w_gate[0], w_up[0], w_down[0]]
    gathered = exchange([tokens] * count, "dev", count)
    other_weights = [lax.ppermute(w, "role", swap) for w in own_weights]

    ids = jnp.pad(expert_ids.astype(BF16), ((0, 0), (0, LANES - picks)), constant_values=-1)
    frequency = rope_base ** (-jnp.arange(dim // 2, dtype=F32) / (dim // 2))
    angles = lengths.astype(F32)[:, None] * frequency[None, :]
    cosine, sine = jnp.cos(angles), jnp.sin(angles)
    cosine = jnp.concatenate([cosine, cosine], axis=1)
    sine = jnp.concatenate([-sine, sine], axis=1)
    visible = jnp.arange(places, dtype=jnp.int32)[None, :] < lengths[:, None]
    bias = jnp.where(visible, 0.0, -jnp.inf).astype(F32)

    messages = call(
        functools.partial(project_kernel, count),
        [((rows, query_width + kv_width + LANES), BF16)] * count,
        [VMEM] * (count + 4),
        [*gathered, norm_gain.reshape(1, -1), w_query, w_keyvalue, ids],
        limit=16 << 20,
    )
    messages = exchange(messages, "dev", count)
    mixtures = call(
        functools.partial(attend_kernel, count),
        [((rows, query_width), BF16)] * count,
        [SMEM] + [VMEM] * (count + 7),
        [dev.reshape(1), *messages, q_gain.reshape(1, -1), k_gain.reshape(1, -1), cosine, sine, bias]
        + [cache_keys, cache_values],
        scratch=[
            pltpu.VMEM((count, rows * group, dim), F32),
            pltpu.VMEM((heads, rows, dim), F32),
            pltpu.VMEM((heads, rows, dim), F32),
            pltpu.VMEM((count, rows, kv_width), F32),
            pltpu.VMEM((rows * group, dim), F32),
        ],
        limit=24 << 20,
    )
    [choice] = call(
        functools.partial(route_kernel, count, groups, capacity, stride),
        [((count * rows, groups * stride), BF16)],
        [SMEM] + [VMEM] * count,
        [jnp.stack([dev, grp])] + [m[:, query_width + kv_width :] for m in messages],
        limit=8 << 20,
    )
    mixtures = exchange(mixtures, "dev", count)
    partials = call(
        functools.partial(out_kernel, count),
        [((rows, width), F32)] + [((rows, width), BF16)] * (count - 1),
        [VMEM] * (count + 1),
        [*mixtures, w_out],
        limit=16 << 20,
    )
    partials = exchange(partials, "dev", count)
    hidden, ready = call(
        functools.partial(ready_kernel, count),
        [((rows, width), F32), ((rows, width), BF16)],
        [VMEM] * (count + 2),
        [*partials, tokens, post_gain.reshape(1, -1)],
        limit=8 << 20,
    )
    ready = exchange([ready] * count, "dev", count)
    packed = call(
        functools.partial(pack_kernel, count),
        [((stride, width), BF16)] * groups,
        [VMEM] * (count + 1),
        [*ready, choice],
        limit=12 << 20,
    )
    packed = exchange(packed, "grp", groups)
    results = call(
        functools.partial(expert_kernel, groups),
        [((stride, width), BF16)] * groups,
        [VMEM] * (groups + 6),
        [*packed, *own_weights, *other_weights],
        limit=32 << 20,
    )
    results = exchange(results, "grp", groups)
    sums = call(
        functools.partial(combine_kernel, groups),
        [((rows, width), F32)] + [((rows, width), BF16)] * (count - 1),
        [VMEM] * (groups + 1),
        [*results, choice],
        limit=12 << 20,
    )
    sums = exchange(sums, "dev", count)
    [output] = call(
        functools.partial(final_kernel, count, picks),
        [((rows, width), BF16)],
        [VMEM] * (count + 1),
        [*sums, hidden],
        limit=8 << 20,
    )
    return output


def rms_scale(values, gain):
    widened = values.astype(jnp.float32)
    mean_square = jnp.mean(widened * widened, axis=-1, keepdims=True)
    return widened * lax.rsqrt(mean_square + epsilon) * gain


def rotate(values, positions):
    half_dim = values.shape[-1] // 2
    frequency = rope_base ** (-jnp.arange(half_dim, dtype=jnp.float32) / half_dim)
    angles = positions.astype(jnp.float32)[:, None, None] * frequency[None, None, :]
    cosine = jnp.cos(angles)
    sine_part = jnp.sin(angles)
    first_half = values[..., :half_dim]
    second_half = values[..., half_dim:]
    return jnp.concatenate(
        [
            first_half * cosine - second_half * sine_part,
            second_half * cosine + first_half * sine_part,
        ],
        axis=-1,
    )


def attend(queries, fresh_kv, cache_keys, cache_values, lengths, q_gain, k_gain):
    batch_rows = queries.shape[0]
    kv_heads = cache_keys.shape[1]
    cache_len = cache_keys.shape[2]
    head_dim = cache_keys.shape[3]
    head_count = queries.shape[1] // head_dim
    group_size = head_count // kv_heads
    scaled_q = rotate(
        rms_scale(queries.reshape(batch_rows, head_count, head_dim), q_gain), lengths
    ).astype(jnp.bfloat16)
    fresh_keys = fresh_kv[:, : kv_heads * head_dim].reshape(batch_rows, kv_heads, head_dim)
    fresh_values = fresh_kv[:, kv_heads * head_dim :].reshape(batch_rows, kv_heads, head_dim)
    scaled_k = rotate(rms_scale(fresh_keys, k_gain), lengths).astype(jnp.bfloat16)
    grouped = scaled_q.reshape(batch_rows, kv_heads, group_size, head_dim)
    factor = head_dim ** (-0.5)
    old_scores = (
        jnp.einsum("rgqd,rgkd->rgqk", grouped, cache_keys, preferred_element_type=jnp.float32)
        * factor
    )
    new_scores = (
        jnp.einsum("rgqd,rgd->rgq", grouped, scaled_k, preferred_element_type=jnp.float32) * factor
    )
    visible = jnp.arange(cache_len, dtype=jnp.int32)[None, :] < lengths[:, None]
    old_scores = jnp.where(visible[:, None, None, :], old_scores, -jnp.inf)
    highest = jnp.maximum(jnp.max(old_scores, axis=-1), new_scores)
    old_weights = jnp.exp(old_scores - highest[..., None])
    new_weights = jnp.exp(new_scores - highest)
    denominator = jnp.sum(old_weights, axis=-1) + new_weights
    old_weights = (old_weights / denominator[..., None]).astype(jnp.bfloat16)
    new_weights = (new_weights / denominator).astype(jnp.bfloat16)
    mixture = jnp.einsum(
        "rgqk,rgkd->rgqd", old_weights, cache_values, preferred_element_type=jnp.float32
    )
    mixture = (
        mixture
        + new_weights.astype(jnp.float32)[..., None]
        * fresh_values.astype(jnp.float32)[:, :, None, :]
    )
    return mixture.reshape(batch_rows, head_count * head_dim).astype(jnp.bfloat16)


def expert_rows(inputs, gate_w, up_w, down_w):
    gate_part = jnp.dot(inputs, gate_w, preferred_element_type=jnp.float32)
    upper_part = jnp.dot(inputs, up_w, preferred_element_type=jnp.float32)
    activated = (jax.nn.silu(gate_part) * upper_part).astype(jnp.bfloat16)
    return jnp.dot(activated, down_w, preferred_element_type=jnp.float32)


def general_body(
    tokens,
    norm_gain,
    q_gain,
    k_gain,
    post_gain,
    w_query,
    w_keyvalue,
    w_out,
    cache_keys,
    cache_values,
    lengths,
    expert_ids,
    w_gate,
    w_up,
    w_down,
):
    normed = rms_scale(tokens, norm_gain).astype(jnp.bfloat16)
    query_width = w_query.shape[1]
    piece = lax.all_gather(normed, "dev", axis=0, tiled=True)
    joined = jnp.concatenate(
        [
            jnp.dot(piece, w_query, preferred_element_type=jnp.float32),
            jnp.dot(piece, w_keyvalue, preferred_element_type=jnp.float32),
        ],
        axis=1,
    )
    projected = joined.astype(jnp.bfloat16)
    queries, fresh_kv = (
        lax.all_to_all(projected[:, :query_width], "dev", split_axis=0, concat_axis=1, tiled=True),
        lax.all_to_all(projected[:, query_width:], "dev", split_axis=0, concat_axis=1, tiled=True),
    )
    mixture = attend(queries, fresh_kv, cache_keys, cache_values, lengths, q_gain, k_gain)
    head_rows = lax.all_to_all(mixture, "dev", split_axis=1, concat_axis=0, tiled=True)
    own_rows = tokens.shape[0]
    attended = lax.psum_scatter(
        jnp.dot(head_rows, w_out, preferred_element_type=jnp.float32).astype(jnp.bfloat16),
        "dev",
        scatter_dimension=0,
        tiled=True,
    ).astype(jnp.float32)
    hidden = tokens.astype(jnp.float32) + attended
    ready = rms_scale(hidden, post_gain).astype(jnp.bfloat16)
    picks = expert_ids.shape[1]
    group_count = lax.axis_size("grp")
    member_count = lax.axis_size("dev")
    expert_count = group_count * member_count
    capacity = min(own_rows, max(3, (own_rows * picks + expert_count - 1) // expert_count + 1))
    model_width = tokens.shape[1]
    flat_ids = expert_ids.reshape(own_rows * picks)
    order_index = jnp.arange(own_rows * picks, dtype=jnp.int32)
    earlier = (flat_ids[:, None] == flat_ids[None, :]) & (
        order_index[None, :] < order_index[:, None]
    )
    slot_index = jnp.sum(earlier.astype(jnp.int32), axis=1)
    position = (flat_ids * capacity + slot_index).reshape(own_rows, picks)
    buffer_rows = jnp.arange(expert_count * capacity, dtype=jnp.int32)
    placing = jnp.any(position[None, :, :] == buffer_rows[:, None, None], axis=2).astype(
        jnp.bfloat16
    )
    outgoing = jnp.dot(placing, ready, preferred_element_type=jnp.float32).astype(jnp.bfloat16)
    arrived = lax.all_to_all(
        outgoing.reshape(expert_count, capacity, model_width),
        ("grp", "dev"),
        split_axis=0,
        concat_axis=0,
        tiled=True,
    )
    arrived = arrived.reshape(expert_count * capacity, model_width)
    full_gate, full_up, full_down = (
        lax.all_gather(w_gate, "role", axis=2, tiled=True),
        lax.all_gather(w_up, "role", axis=2, tiled=True),
        lax.all_gather(w_down, "role", axis=1, tiled=True),
    )
    expert_out = expert_rows(arrived, full_gate[0], full_up[0], full_down[0]).astype(jnp.bfloat16)
    returned = lax.all_to_all(
        expert_out.reshape(expert_count, capacity, model_width),
        ("grp", "dev"),
        split_axis=0,
        concat_axis=0,
        tiled=True,
    )
    returned = returned.reshape(expert_count * capacity, model_width)
    selected = (
        jnp.take(returned, position.reshape(own_rows * picks), axis=0)
        .astype(jnp.float32)
        .reshape(own_rows, picks, model_width)
    )
    output = hidden + jnp.sum(selected, axis=1) / picks
    return output.astype(jnp.bfloat16)


def solution(mesh):
    sizes = dict(mesh.shape)

    def step(*args):
        heads = args[8].shape[1]
        powers = all(sizes[axis] & (sizes[axis] - 1) == 0 for axis in ("grp", "dev"))
        fitted = sizes["dev"] == heads and sizes["role"] == 2 and powers
        return (body if fitted else general_body)(*args)

    return jax.shard_map(
        step,
        mesh=mesh,
        in_specs=(
            P(("role", "grp", "dev"), None),
            P(),
            P(),
            P(),
            P(),
            P(None, "dev"),
            P(None, "dev"),
            P("dev", None),
            P(("role", "grp", "dev"), None, None, None),
            P(("role", "grp", "dev"), None, None, None),
            P(("role", "grp", "dev")),
            P(("role", "grp", "dev"), None),
            P(("grp", "dev"), None, "role"),
            P(("grp", "dev"), None, "role"),
            P(("grp", "dev"), "role", None),
        ),
        out_specs=P(("role", "grp", "dev"), None),
        check_vma=False,
    )
```

```python
import functools

import jax
import jax.numpy as jnp
from jax import lax
from jax.experimental import pallas as pl
from jax.experimental.pallas import tpu as pltpu
from jax.sharding import PartitionSpec as P


epsilon = 1e-06
rope_base = 1000000.0
LANES = 128
VMEM = pl.BlockSpec(memory_space=pltpu.VMEM)
SMEM = pl.BlockSpec(memory_space=pltpu.SMEM)
ANY = pl.BlockSpec(memory_space=pl.ANY)
F32 = jnp.float32
BF16 = jnp.bfloat16


def call(kernel, outs, specs, args, scratch=(), cost=None, limit=None, kept=True):
    flops, moved = cost or (0, 0)
    place = pltpu.VMEM if kept else jax.ShapeDtypeStruct
    return pl.pallas_call(
        kernel,
        out_shape=[place(shape, dtype) for shape, dtype in outs],
        in_specs=list(specs),
        out_specs=[VMEM] * len(outs),
        scratch_shapes=list(scratch),
        cost_estimate=pl.CostEstimate(flops=flops, bytes_accessed=moved, transcendentals=0),
        compiler_params=pltpu.CompilerParams(vmem_limit_bytes=limit),
    )(*args)


def exchange(pieces, axis, size):
    got = [pieces[0]]
    for step in range(1, size):
        got.append(lax.ppermute(pieces[step], axis, [(i, i ^ step) for i in range(size)]))
    return got


def fetch_kernel(count, _, *refs):
    sources, targets, sems = refs[:count], refs[count : 2 * count], refs[2 * count]
    copies = [pltpu.make_async_copy(a, b, sems.at[i]) for i, (a, b) in enumerate(zip(sources, targets))]
    for copy in copies:
        copy.start()
    for copy in copies:
        copy.wait()


def fetch(after, *arrays, held=True):
    moved = sum(a.size * a.dtype.itemsize for a in arrays)
    return call(
        functools.partial(fetch_kernel, len(arrays)),
        [(a.shape, a.dtype) for a in arrays],
        [SMEM] + [ANY] * len(arrays),
        [after] + [pltpu.with_memory_space_constraint(a, pltpu.HBM) if held else a for a in arrays],
        scratch=[pltpu.SemaphoreType.DMA((len(arrays),))],
        cost=(0, moved),
        limit=1 << 20,
    )


def rms(values, gain):
    mean_square = jnp.mean(values * values, axis=-1, keepdims=True)
    return values * lax.rsqrt(mean_square + epsilon) * gain


def stack(refs):
    return jnp.concatenate([ref[...].astype(F32) for ref in refs], axis=0)


def project_kernel(count, *refs):
    blocks, (gain, w_query, w_keyvalue, ids), outs = refs[:count], refs[count : count + 4], refs[count + 4 :]
    rows = blocks[0].shape[0]
    query_width = w_query.shape[1]
    kv_width = w_keyvalue.shape[1]
    normed = rms(stack(blocks), gain[...]).astype(BF16)
    queries = jnp.dot(normed, w_query[...], preferred_element_type=F32)
    fresh = jnp.dot(normed, w_keyvalue[...], preferred_element_type=F32)
    for step in range(count):
        own = slice(step * rows, (step + 1) * rows)
        outs[step][:, :query_width] = queries[own].astype(BF16)
        outs[step][:, query_width : query_width + kv_width] = fresh[own].astype(BF16)
        outs[step][:, query_width + kv_width :] = ids[...]


def turn(values, gain, cosine, sine):
    values = rms(values, gain)
    return values * cosine + pltpu.roll(values, values.shape[1] // 2, 1) * sine


def attend_cache(message, head, gain, cosine, sine, bias, keys, values, scratch):
    rows, _, _, dim = keys.shape
    group = scratch.shape[0] // rows
    for h in range(group):
        piece = message[:, h * dim : (h + 1) * dim].astype(F32)
        scratch[pl.ds(h, rows, stride=group), :] = turn(piece, gain, cosine, sine)
    query = scratch[...].reshape(rows, group, dim).astype(BF16)
    scores = jnp.einsum("rqd,rkd->rqk", query, keys[:, head], preferred_element_type=F32) * dim ** (-0.5)
    scores = scores + bias[:, None, :]
    top = jnp.max(scores, axis=-1, keepdims=True)
    weights = jnp.exp(scores - top)
    total = jnp.sum(weights, axis=-1, keepdims=True)
    mixed = jnp.einsum("rqk,rkd->rqd", weights.astype(BF16), values[:, head], preferred_element_type=F32)
    return query.astype(F32), top, total, mixed


def attend_kernel(steps, me_ref, *refs):
    count = len(steps)
    messages = refs[:count]
    gain, cosine, sine, bias, keys, values = refs[count : count + 6]
    outs, scratch = refs[count + 7 : -1], refs[-1]
    for i, step in enumerate(steps):
        found = attend_cache(
            messages[i], me_ref[0] ^ step, gain[...], cosine[...], sine[...], bias[...], keys, values, scratch.at[i]
        )
        for out, value in zip(outs[4 * i : 4 * i + 4], found):
            out[...] = jnp.broadcast_to(value, out.shape)


def mix_kernel(count, done, me_ref, *refs):
    messages, parts = refs[:count], refs[count : count + 4 * done]
    refs = refs[count + 4 * done :]
    q_gain, k_gain, cosine, sine, bias, keys, values = refs[:7]
    outs = refs[7 : 7 + count]
    scratch, k_rot, v_new, kv_all = refs[7 + count :]
    me = me_ref[0]
    rows, heads, _, dim = keys.shape
    group = scratch.shape[1] // rows
    query_width = group * dim
    kv_width = kv_all.shape[2]
    cos, sin = cosine[...], sine[...]
    last = [
        attend_cache(messages[step], me ^ step, q_gain[...], cos, sin, bias[...], keys, values, scratch.at[step])
        for step in range(done, count)
    ]
    for step in range(count):
        kv_all[me ^ step] = messages[step][:, query_width : query_width + kv_width].astype(F32)
    for h in range(2 * heads):
        column = h * dim
        piece = kv_all[column // kv_width, :, column % kv_width : column % kv_width + dim]
        if h < heads:
            k_rot[h] = turn(piece, k_gain[...], cos, sin).astype(BF16).astype(F32)
        else:
            v_new[h - heads] = piece
    for step in reversed(range(count)):
        head = me ^ step
        if step < done:
            query, top, total, mixed = [ref[...] for ref in parts[4 * step : 4 * step + 4]]
            top, total = top[:, :, :1], total[:, :, :1]
        else:
            query, top, total, mixed = last[step - done]
        new = jnp.sum(query * k_rot[head][:, None, :], axis=-1, keepdims=True) * dim ** (-0.5)
        highest = jnp.maximum(top, new)
        old = jnp.exp(top - highest)
        new = jnp.exp(new - highest)
        share = 1.0 / (total * old + new)
        out = mixed * (old * share) + (new * share) * v_new[head][:, None, :]
        scratch[step] = out.reshape(rows * group, dim)
        for h in range(group):
            outs[step][:, h * dim : (h + 1) * dim] = scratch[step, pl.ds(h, rows, stride=group), :].astype(BF16)


def out_kernel(count, *refs):
    blocks, w_out, outs = refs[:count], refs[count], refs[count + 1 :]
    rows = blocks[0].shape[0]
    partial = jnp.dot(stack(blocks).astype(BF16), w_out[...], preferred_element_type=F32)
    for step in range(count):
        outs[step][...] = partial[step * rows : (step + 1) * rows].astype(outs[step].dtype)


def ready_kernel(count, *refs):
    blocks, (tokens, gain), (hidden, ready) = refs[:count], refs[count : count + 2], refs[count + 2 :]
    total = blocks[0][...]
    for block in blocks[1:]:
        total = total + block[...].astype(F32)
    total = tokens[...].astype(F32) + total
    hidden[...] = total
    ready[...] = rms(total, gain[...]).astype(BF16)


def route_kernel(count, groups, capacity, where_ref, *refs):
    messages, outs = refs[:count], refs[count:]
    dev, grp = where_ref[0], where_ref[1]
    rows, columns = messages[0].shape
    total = count * rows
    lane = lax.broadcasted_iota(jnp.int32, (total, LANES), 1)
    down = lax.broadcasted_iota(jnp.int32, (total, total), 0)
    across = lax.broadcasted_iota(jnp.int32, (total, total), 1)
    earlier = jnp.where((across < down) & (across // rows == down // rows), 1.0, 0.0).astype(BF16)
    table = jnp.concatenate([m[:, columns - LANES :].astype(F32) for m in messages], axis=0)
    named = jnp.zeros((total, LANES), F32)
    for step in range(groups):
        expert = ((grp ^ step) * count + dev).astype(F32)
        hit = jnp.max(jnp.where(table == expert, 1.0, 0.0), axis=1, keepdims=True)
        named = jnp.where(lane == step, hit, named)
    rank = jnp.dot(earlier, named.astype(BF16), preferred_element_type=F32)
    source = (lax.broadcasted_iota(jnp.int32, (total, LANES), 0) // rows).astype(F32)
    slot = rank + source * capacity
    first = 0
    for out in outs:
        held = out.shape[0]
        stride = out.shape[1] // groups
        place = lax.broadcasted_iota(jnp.int32, out.shape, 1).astype(F32)
        chosen = jnp.zeros(out.shape, F32)
        for step in range(groups):
            at = slot[:held, step : step + 1] - first
            inside = (at >= 0) & (at < stride) & (named[:held, step : step + 1] > 0)
            chosen = jnp.where((place == at + step * stride) & inside, 1.0, chosen)
        out[...] = chosen.astype(BF16)
        first += stride


def pack_kernel(count, *refs):
    blocks, choice, outs = refs[:count], refs[count], refs[count + 2 :]
    stride = outs[0].shape[0]
    packed = lax.dot_general(
        choice[...], stack(blocks).astype(BF16), (((0,), (0,)), ((), ())), preferred_element_type=F32
    )
    for step, out in enumerate(outs):
        out[...] = packed[step * stride : (step + 1) * stride].astype(BF16)


def expert_kernel(groups, *refs):
    blocks, weights, outs = refs[:groups], refs[groups : groups + 6], refs[groups + 6 :]
    stride = outs[0].shape[0]
    inputs = stack(blocks).astype(BF16)
    total = None
    for half in range(2):
        gate, up, down = weights[3 * half : 3 * half + 3]
        gated = jnp.dot(inputs, gate[...], preferred_element_type=F32)
        upper = jnp.dot(inputs, up[...], preferred_element_type=F32)
        active = (gated / (1.0 + jnp.exp(-gated)) * upper).astype(BF16)
        part = jnp.dot(active, down[...], preferred_element_type=F32)
        total = part if total is None else total + part
    for step, out in enumerate(outs):
        out[...] = total[step * stride : (step + 1) * stride].astype(BF16)


def combine_kernel(groups, sets, start, *refs):
    choices, outs = refs[sets * groups : sets * (groups + 1)], refs[sets * (groups + 1) + 1 :]
    rows = outs[0].shape[0]
    summed = None
    for i, choice in enumerate(choices):
        part = jnp.dot(
            choice[start : start + len(outs) * rows],
            stack(refs[i * groups : (i + 1) * groups]).astype(BF16),
            preferred_element_type=F32,
        )
        summed = part if summed is None else summed + part
    for step, out in enumerate(outs):
        out[...] = summed[step * rows : (step + 1) * rows].astype(out.dtype)


def final_kernel(count, picks, *refs):
    blocks, hidden, out = refs[:count], refs[count], refs[count + 1]
    total = blocks[0][...]
    for block in blocks[1:]:
        total = total + block[...].astype(F32)
    out[...] = (hidden[...] + total / picks).astype(BF16)


def body(
    tokens,
    norm_gain,
    q_gain,
    k_gain,
    post_gain,
    w_query,
    w_keyvalue,
    w_out,
    cache_keys,
    cache_values,
    lengths,
    expert_ids,
    w_gate,
    w_up,
    w_down,
):
    count, groups = lax.axis_size("dev"), lax.axis_size("grp")
    rows, width = tokens.shape
    picks = expert_ids.shape[1]
    heads, places, dim = cache_keys.shape[1:]
    query_width, kv_width = w_query.shape[1], w_keyvalue.shape[1]
    group = query_width // dim
    experts = count * groups
    capacity = min(rows, max(3, (rows * picks + experts - 1) // experts + 1))
    strides = [max(8, count // 2 * capacity // 8 * 8)]
    strides.append(max(8, -(-(count * capacity - strides[0]) // 8) * 8))
    where = jnp.stack([lax.axis_index("dev"), lax.axis_index("grp")])

    half = count // 2
    near, far = list(range(half)), list(range(half, count))
    swap = [(0, 1), (1, 0)]
    own_weights = [w_gate[0], w_up[0], w_down[0]]
    gathered = exchange([tokens] * count, "dev", count)
    other_weights = [lax.ppermute(w, "role", swap) for w in own_weights]
    query_kept, kv_kept, tokens_kept, gain_kept = fetch(where, w_query, w_keyvalue, tokens, norm_gain.reshape(1, -1))
    gathered[0] = tokens_kept

    ids = jnp.pad(expert_ids.astype(BF16), ((0, 0), (0, LANES - picks)), constant_values=-1)
    frequency = rope_base ** (-jnp.arange(dim // 2, dtype=F32) / (dim // 2))
    angles = lengths.astype(F32)[:, None] * frequency[None, :]
    cosine, sine = jnp.cos(angles), jnp.sin(angles)
    cosine = jnp.concatenate([cosine, cosine], axis=1)
    sine = jnp.concatenate([-sine, sine], axis=1)
    visible = jnp.arange(places, dtype=jnp.int32)[None, :] < lengths[:, None]
    bias = jnp.where(visible, 0.0, -jnp.inf).astype(F32)

    chunks = [near, far]
    messages = [None] * count
    for chunk in chunks:
        made = call(
            functools.partial(project_kernel, len(chunk)),
            [((rows, query_width + kv_width + LANES), BF16)] * len(chunk),
            [VMEM] * (len(chunk) + 4),
            [*[gathered[step] for step in chunk], gain_kept, query_kept, kv_kept, ids],
            cost=(2 * len(chunk) * rows * width * (query_width + kv_width), 3 << 20),
            limit=4 << 20,
        )
        for step, message in zip(chunk, made):
            messages[step] = message
    messages = exchange(messages, "dev", count)
    parts = []
    gains = [q_gain.reshape(1, -1), k_gain.reshape(1, -1)]
    flops = 4 * rows * group * places * dim
    for chunk in chunks[:-1]:
        parts += call(
            functools.partial(attend_kernel, chunk),
            [((rows, group, dim), F32)] * (4 * len(chunk)),
            [SMEM] + [VMEM] * (len(chunk) + 6) + [ANY],
            [where, *[messages[step] for step in chunk], gains[0], cosine, sine, bias]
            + [cache_keys, cache_values, parts[-1] if parts else bias],
            scratch=[pltpu.VMEM((len(chunk), rows * group, dim), F32)],
            cost=(len(chunk) * flops, 2 << 20),
            limit=4 << 20,
        )
    mixtures = call(
        functools.partial(mix_kernel, count, half),
        [((rows, query_width), BF16)] * count,
        [SMEM] + [VMEM] * (count + 4 * half + 7),
        [where, *messages, *parts, *gains, cosine, sine, bias, cache_keys, cache_values],
        scratch=[
            pltpu.VMEM((count, rows * group, dim), F32),
            pltpu.VMEM((heads, rows, dim), F32),
            pltpu.VMEM((heads, rows, dim), F32),
            pltpu.VMEM((count, rows, kv_width), F32),
        ],
        cost=(flops, 2 << 20),
        limit=4 << 20,
    )
    choices = call(
        functools.partial(route_kernel, count, groups, capacity),
        [((half * rows, groups * strides[0]), BF16), ((count * rows, groups * strides[1]), BF16)],
        [SMEM] + [VMEM] * count,
        [where, *messages],
        cost=(0, 2 << 20),
        limit=2 << 20,
    )
    mixtures = exchange(mixtures, "dev", count)
    partials = [None] * count
    for chunk in chunks:
        made = call(
            functools.partial(out_kernel, len(chunk)),
            [((rows, width), BF16 if step else F32) for step in chunk],
            [VMEM] * (len(chunk) + 1),
            [*[mixtures[step] for step in chunk], w_out],
            cost=(2 * len(chunk) * rows * width * query_width, 2 << 20),
            limit=4 << 20,
        )
        for step, partial in zip(chunk, made):
            partials[step] = partial
    partials = exchange(partials, "dev", count)
    hidden, ready = call(
        functools.partial(ready_kernel, count),
        [((rows, width), F32), ((rows, width), BF16)],
        [VMEM] * (count + 2),
        [*partials, tokens_kept, post_gain.reshape(1, -1)],
        cost=(0, 1 << 20),
        limit=8 << 20,
    )
    ready = exchange([ready] * count, "dev", count)
    other_weights = fetch(where, *other_weights, held=False)
    results = []
    after = hidden
    for part, choice, stride in zip((near, near + far), choices, strides):
        packed = call(
            functools.partial(pack_kernel, len(part)),
            [((stride, width), BF16)] * groups,
            [VMEM] * (len(part) + 1) + [ANY],
            [*[ready[step] for step in part], choice, after],
            cost=(0, 1 << 20),
            limit=4 << 20,
        )
        after = packed[0]
        packed = exchange(packed, "grp", groups)
        results.append(
            call(
                functools.partial(expert_kernel, groups),
                [((stride, width), BF16)] * groups,
                [VMEM] * (groups + 6),
                [*packed, *own_weights, *other_weights],
                cost=(6 * groups * stride * width * w_gate.shape[2] * 2, 4 << 20),
                limit=8 << 20,
            )
        )
    results = lax.optimization_barrier(results)
    sums = [None] * count
    after = hidden
    held = [None, exchange(results[1], "grp", groups)]
    held[0] = exchange(results[0], "grp", groups)
    for part, used in ((far, [1]), (near, [0, 1])):
        made = call(
            functools.partial(combine_kernel, groups, len(used), part[0] * rows),
            [((rows, width), BF16 if step else F32) for step in part],
            [VMEM] * (len(used) * (groups + 1)) + [ANY],
            [*sum([held[i] for i in used], []), *[choices[i] for i in used], after],
            cost=(0, 1 << 20),
            limit=4 << 20,
        )
        after = made[0]
        for step, total in zip(part, made):
            sums[step] = total
    sums = exchange(sums, "dev", count)
    [output] = call(
        functools.partial(final_kernel, count, picks),
        [((rows, width), BF16)],
        [VMEM] * (count + 1),
        [*sums, hidden],
        cost=(0, 1 << 20),
        limit=8 << 20,
        kept=False,
    )
    return output


def rms_scale(values, gain):
    widened = values.astype(jnp.float32)
    mean_square = jnp.mean(widened * widened, axis=-1, keepdims=True)
    return widened * lax.rsqrt(mean_square + epsilon) * gain


def rotate(values, positions):
    half_dim = values.shape[-1] // 2
    frequency = rope_base ** (-jnp.arange(half_dim, dtype=jnp.float32) / half_dim)
    angles = positions.astype(jnp.float32)[:, None, None] * frequency[None, None, :]
    cosine = jnp.cos(angles)
    sine_part = jnp.sin(angles)
    first_half = values[..., :half_dim]
    second_half = values[..., half_dim:]
    return jnp.concatenate(
        [
            first_half * cosine - second_half * sine_part,
            second_half * cosine + first_half * sine_part,
        ],
        axis=-1,
    )


def attend(queries, fresh_kv, cache_keys, cache_values, lengths, q_gain, k_gain):
    batch_rows = queries.shape[0]
    kv_heads = cache_keys.shape[1]
    cache_len = cache_keys.shape[2]
    head_dim = cache_keys.shape[3]
    head_count = queries.shape[1] // head_dim
    group_size = head_count // kv_heads
    scaled_q = rotate(
        rms_scale(queries.reshape(batch_rows, head_count, head_dim), q_gain), lengths
    ).astype(jnp.bfloat16)
    fresh_keys = fresh_kv[:, : kv_heads * head_dim].reshape(batch_rows, kv_heads, head_dim)
    fresh_values = fresh_kv[:, kv_heads * head_dim :].reshape(batch_rows, kv_heads, head_dim)
    scaled_k = rotate(rms_scale(fresh_keys, k_gain), lengths).astype(jnp.bfloat16)
    grouped = scaled_q.reshape(batch_rows, kv_heads, group_size, head_dim)
    factor = head_dim ** (-0.5)
    old_scores = (
        jnp.einsum("rgqd,rgkd->rgqk", grouped, cache_keys, preferred_element_type=jnp.float32)
        * factor
    )
    new_scores = (
        jnp.einsum("rgqd,rgd->rgq", grouped, scaled_k, preferred_element_type=jnp.float32) * factor
    )
    visible = jnp.arange(cache_len, dtype=jnp.int32)[None, :] < lengths[:, None]
    old_scores = jnp.where(visible[:, None, None, :], old_scores, -jnp.inf)
    highest = jnp.maximum(jnp.max(old_scores, axis=-1), new_scores)
    old_weights = jnp.exp(old_scores - highest[..., None])
    new_weights = jnp.exp(new_scores - highest)
    denominator = jnp.sum(old_weights, axis=-1) + new_weights
    old_weights = (old_weights / denominator[..., None]).astype(jnp.bfloat16)
    new_weights = (new_weights / denominator).astype(jnp.bfloat16)
    mixture = jnp.einsum(
        "rgqk,rgkd->rgqd", old_weights, cache_values, preferred_element_type=jnp.float32
    )
    mixture = (
        mixture
        + new_weights.astype(jnp.float32)[..., None]
        * fresh_values.astype(jnp.float32)[:, :, None, :]
    )
    return mixture.reshape(batch_rows, head_count * head_dim).astype(jnp.bfloat16)


def expert_rows(inputs, gate_w, up_w, down_w):
    gate_part = jnp.dot(inputs, gate_w, preferred_element_type=jnp.float32)
    upper_part = jnp.dot(inputs, up_w, preferred_element_type=jnp.float32)
    activated = (jax.nn.silu(gate_part) * upper_part).astype(jnp.bfloat16)
    return jnp.dot(activated, down_w, preferred_element_type=jnp.float32)


def general_body(
    tokens,
    norm_gain,
    q_gain,
    k_gain,
    post_gain,
    w_query,
    w_keyvalue,
    w_out,
    cache_keys,
    cache_values,
    lengths,
    expert_ids,
    w_gate,
    w_up,
    w_down,
):
    normed = rms_scale(tokens, norm_gain).astype(jnp.bfloat16)
    query_width = w_query.shape[1]
    piece = lax.all_gather(normed, "dev", axis=0, tiled=True)
    joined = jnp.concatenate(
        [
            jnp.dot(piece, w_query, preferred_element_type=jnp.float32),
            jnp.dot(piece, w_keyvalue, preferred_element_type=jnp.float32),
        ],
        axis=1,
    )
    projected = joined.astype(jnp.bfloat16)
    queries, fresh_kv = (
        lax.all_to_all(projected[:, :query_width], "dev", split_axis=0, concat_axis=1, tiled=True),
        lax.all_to_all(projected[:, query_width:], "dev", split_axis=0, concat_axis=1, tiled=True),
    )
    mixture = attend(queries, fresh_kv, cache_keys, cache_values, lengths, q_gain, k_gain)
    head_rows = lax.all_to_all(mixture, "dev", split_axis=1, concat_axis=0, tiled=True)
    own_rows = tokens.shape[0]
    attended = lax.psum_scatter(
        jnp.dot(head_rows, w_out, preferred_element_type=jnp.float32).astype(jnp.bfloat16),
        "dev",
        scatter_dimension=0,
        tiled=True,
    ).astype(jnp.float32)
    hidden = tokens.astype(jnp.float32) + attended
    ready = rms_scale(hidden, post_gain).astype(jnp.bfloat16)
    picks = expert_ids.shape[1]
    group_count = lax.axis_size("grp")
    member_count = lax.axis_size("dev")
    expert_count = group_count * member_count
    capacity = min(own_rows, max(3, (own_rows * picks + expert_count - 1) // expert_count + 1))
    model_width = tokens.shape[1]
    flat_ids = expert_ids.reshape(own_rows * picks)
    order_index = jnp.arange(own_rows * picks, dtype=jnp.int32)
    earlier = (flat_ids[:, None] == flat_ids[None, :]) & (
        order_index[None, :] < order_index[:, None]
    )
    slot_index = jnp.sum(earlier.astype(jnp.int32), axis=1)
    position = (flat_ids * capacity + slot_index).reshape(own_rows, picks)
    buffer_rows = jnp.arange(expert_count * capacity, dtype=jnp.int32)
    placing = jnp.any(position[None, :, :] == buffer_rows[:, None, None], axis=2).astype(
        jnp.bfloat16
    )
    outgoing = jnp.dot(placing, ready, preferred_element_type=jnp.float32).astype(jnp.bfloat16)
    arrived = lax.all_to_all(
        outgoing.reshape(expert_count, capacity, model_width),
        ("grp", "dev"),
        split_axis=0,
        concat_axis=0,
        tiled=True,
    )
    arrived = arrived.reshape(expert_count * capacity, model_width)
    full_gate, full_up, full_down = (
        lax.all_gather(w_gate, "role", axis=2, tiled=True),
        lax.all_gather(w_up, "role", axis=2, tiled=True),
        lax.all_gather(w_down, "role", axis=1, tiled=True),
    )
    expert_out = expert_rows(arrived, full_gate[0], full_up[0], full_down[0]).astype(jnp.bfloat16)
    returned = lax.all_to_all(
        expert_out.reshape(expert_count, capacity, model_width),
        ("grp", "dev"),
        split_axis=0,
        concat_axis=0,
        tiled=True,
    )
    returned = returned.reshape(expert_count * capacity, model_width)
    selected = (
        jnp.take(returned, position.reshape(own_rows * picks), axis=0)
        .astype(jnp.float32)
        .reshape(own_rows, picks, model_width)
    )
    output = hidden + jnp.sum(selected, axis=1) / picks
    return output.astype(jnp.bfloat16)


def solution(mesh):
    sizes = dict(mesh.shape)

    def step(*args):
        heads = args[8].shape[1]
        powers = all(sizes[axis] & (sizes[axis] - 1) == 0 for axis in ("grp", "dev"))
        fitted = sizes["dev"] == heads and sizes["role"] == 2 and powers
        if not fitted:
            return general_body(*args)
        return body(*args)

    return jax.shard_map(
        step,
        mesh=mesh,
        in_specs=(
            P(("role", "grp", "dev"), None),
            P(),
            P(),
            P(),
            P(),
            P(None, "dev"),
            P(None, "dev"),
            P("dev", None),
            P(("role", "grp", "dev"), None, None, None),
            P(("role", "grp", "dev"), None, None, None),
            P(("role", "grp", "dev")),
            P(("role", "grp", "dev"), None),
            P(("grp", "dev"), None, "role"),
            P(("grp", "dev"), None, "role"),
            P(("grp", "dev"), "role", None),
        ),
        out_specs=P(("role", "grp", "dev"), None),
        check_vma=False,
    )
```

```python
import functools

import jax
import jax.numpy as jnp
from jax import lax
from jax.experimental import pallas as pl
from jax.experimental.pallas import tpu as pltpu
from jax.sharding import PartitionSpec as P


epsilon = 1e-06
rope_base = 1000000.0
LANES = 128
VMEM = pl.BlockSpec(memory_space=pltpu.VMEM)
ANY = pl.BlockSpec(memory_space=pl.ANY)
F32 = jnp.float32
BF16 = jnp.bfloat16


def call(kernel, outs, specs, args, scratch=(), cost=None, limit=None, kept=True):
    flops, moved = cost or (0, 0)
    place = pltpu.VMEM if kept else jax.ShapeDtypeStruct
    return pl.pallas_call(
        kernel,
        out_shape=[place(shape, dtype) for shape, dtype in outs],
        in_specs=list(specs),
        out_specs=[VMEM] * len(outs),
        scratch_shapes=list(scratch),
        cost_estimate=pl.CostEstimate(flops=flops, bytes_accessed=moved, transcendentals=0),
        compiler_params=pltpu.CompilerParams(vmem_limit_bytes=limit),
    )(*args)


def exchange(pieces, axis, size):
    got = [pieces[0]]
    for step in range(1, size):
        got.append(lax.ppermute(pieces[step], axis, [(i, i ^ step) for i in range(size)]))
    return got


def fetch_kernel(count, *refs):
    sources, targets, sems = refs[:count], refs[count : 2 * count], refs[2 * count]
    copies = [pltpu.make_async_copy(a, b, sems.at[i]) for i, (a, b) in enumerate(zip(sources, targets))]
    for copy in copies:
        copy.start()
    for copy in copies:
        copy.wait()


def fetch(*arrays, held=True):
    moved = sum(a.size * a.dtype.itemsize for a in arrays)
    return call(
        functools.partial(fetch_kernel, len(arrays)),
        [(a.shape, a.dtype) for a in arrays],
        [ANY] * len(arrays),
        [pltpu.with_memory_space_constraint(a, pltpu.HBM) if held else a for a in arrays],
        scratch=[pltpu.SemaphoreType.DMA((len(arrays),))],
        cost=(0, moved),
        limit=1 << 20,
    )


def rms(values, gain):
    mean_square = jnp.mean(values * values, axis=-1, keepdims=True)
    return values * lax.rsqrt(mean_square + epsilon) * gain


def stack(refs):
    return jnp.concatenate([ref[...].astype(F32) for ref in refs], axis=0)


def project_kernel(count, *refs):
    blocks, (gain, w_query, w_keyvalue, ids), outs = refs[:count], refs[count : count + 4], refs[count + 4 :]
    rows = blocks[0].shape[0]
    query_width = w_query.shape[1]
    kv_width = w_keyvalue.shape[1]
    picks = ids.shape[0]
    spread = lax.broadcasted_iota(jnp.int32, (picks, LANES), 0) == lax.broadcasted_iota(jnp.int32, (picks, LANES), 1)
    named = lax.dot_general(
        ids[...].astype(F32).astype(BF16),
        jnp.where(spread, 1.0, 0.0).astype(BF16),
        (((0,), (0,)), ((), ())),
        preferred_element_type=F32,
    )
    lane = lax.broadcasted_iota(jnp.int32, named.shape, 1)
    named = jnp.where(lane < picks, named, -1.0).astype(BF16)
    normed = rms(stack(blocks), gain[...]).astype(BF16)
    queries = jnp.dot(normed, w_query[...], preferred_element_type=F32)
    fresh = jnp.dot(normed, w_keyvalue[...], preferred_element_type=F32)
    for step in range(count):
        own = slice(step * rows, (step + 1) * rows)
        outs[step][:, :query_width] = queries[own].astype(BF16)
        outs[step][:, query_width : query_width + kv_width] = fresh[own].astype(BF16)
        outs[step][:, query_width + kv_width :] = named


def turn(values, gain, cosine, sine):
    values = rms(values, gain)
    return values * cosine + pltpu.roll(values, values.shape[1] // 2, 1) * sine


def attend_cache(message, head, gain, cosine, sine, bias, keys, values, scratch):
    rows, _, _, dim = keys.shape
    group = scratch.shape[0] // rows
    for h in range(group):
        piece = message[:, h * dim : (h + 1) * dim].astype(F32)
        scratch[pl.ds(h, rows, stride=group), :] = turn(piece, gain, cosine, sine)
    query = scratch[...].reshape(rows, group, dim).astype(BF16)
    scores = jnp.einsum("rqd,rkd->rqk", query, keys[:, head], preferred_element_type=F32) * dim ** (-0.5)
    scores = scores + bias[:, None, :]
    top = jnp.max(scores, axis=-1, keepdims=True)
    weights = jnp.exp(scores - top)
    total = jnp.sum(weights, axis=-1, keepdims=True)
    mixed = jnp.einsum("rqk,rkd->rqd", weights.astype(BF16), values[:, head], preferred_element_type=F32)
    return query.astype(F32), top, total, mixed


def attend_kernel(steps, *refs):
    count = len(steps)
    me = lax.axis_index("dev")
    messages = refs[:count]
    gain, cosine, sine, bias, keys, values = refs[count : count + 6]
    outs, scratch = refs[count + 7 : -1], refs[-1]
    for i, step in enumerate(steps):
        found = attend_cache(
            messages[i], me ^ step, gain[...], cosine[...], sine[...], bias[...], keys, values, scratch.at[i]
        )
        for out, value in zip(outs[4 * i : 4 * i + 4], found):
            out[...] = jnp.broadcast_to(value, out.shape)


def mix_kernel(count, done, *refs):
    messages, parts = refs[:count], refs[count : count + 4 * done]
    refs = refs[count + 4 * done :]
    q_gain, k_gain, cosine, sine, bias, keys, values = refs[:7]
    outs = refs[7 : 7 + count]
    scratch, k_rot, v_new, kv_all = refs[7 + count :]
    me = lax.axis_index("dev")
    rows, heads, _, dim = keys.shape
    group = scratch.shape[1] // rows
    query_width = group * dim
    kv_width = kv_all.shape[2]
    cos, sin = cosine[...], sine[...]
    last = [
        attend_cache(messages[step], me ^ step, q_gain[...], cos, sin, bias[...], keys, values, scratch.at[step])
        for step in range(done, count)
    ]
    for step in range(count):
        kv_all[me ^ step] = messages[step][:, query_width : query_width + kv_width].astype(F32)
    for h in range(2 * heads):
        column = h * dim
        piece = kv_all[column // kv_width, :, column % kv_width : column % kv_width + dim]
        if h < heads:
            k_rot[h] = turn(piece, k_gain[...], cos, sin).astype(BF16).astype(F32)
        else:
            v_new[h - heads] = piece
    for step in reversed(range(count)):
        head = me ^ step
        if step < done:
            query, top, total, mixed = [ref[...] for ref in parts[4 * step : 4 * step + 4]]
            top, total = top[:, :, :1], total[:, :, :1]
        else:
            query, top, total, mixed = last[step - done]
        new = jnp.sum(query * k_rot[head][:, None, :], axis=-1, keepdims=True) * dim ** (-0.5)
        highest = jnp.maximum(top, new)
        old = jnp.exp(top - highest)
        new = jnp.exp(new - highest)
        share = 1.0 / (total * old + new)
        out = mixed * (old * share) + (new * share) * v_new[head][:, None, :]
        scratch[step] = out.reshape(rows * group, dim)
        for h in range(group):
            outs[step][:, h * dim : (h + 1) * dim] = scratch[step, pl.ds(h, rows, stride=group), :].astype(BF16)


def out_kernel(count, *refs):
    blocks, w_out, outs = refs[:count], refs[count], refs[count + 1 :]
    rows = blocks[0].shape[0]
    partial = jnp.dot(stack(blocks).astype(BF16), w_out[...], preferred_element_type=F32)
    for step in range(count):
        outs[step][...] = partial[step * rows : (step + 1) * rows].astype(outs[step].dtype)


def ready_kernel(count, *refs):
    blocks, (tokens, gain), (hidden, ready) = refs[:count], refs[count : count + 2], refs[count + 2 :]
    total = blocks[0][...]
    for block in blocks[1:]:
        total = total + block[...].astype(F32)
    total = tokens[...].astype(F32) + total
    hidden[...] = total
    ready[...] = rms(total, gain[...]).astype(BF16)


def route_kernel(count, groups, capacity, *refs):
    messages, outs = refs[:count], refs[count:]
    dev, grp = lax.axis_index("dev"), lax.axis_index("grp")
    rows, columns = messages[0].shape
    total = count * rows
    lane = lax.broadcasted_iota(jnp.int32, (total, LANES), 1)
    down = lax.broadcasted_iota(jnp.int32, (total, total), 0)
    across = lax.broadcasted_iota(jnp.int32, (total, total), 1)
    earlier = jnp.where((across < down) & (across // rows == down // rows), 1.0, 0.0).astype(BF16)
    table = jnp.concatenate([m[:, columns - LANES :].astype(F32) for m in messages], axis=0)
    named = jnp.zeros((total, LANES), F32)
    for step in range(groups):
        expert = ((grp ^ step) * count + dev).astype(F32)
        hit = jnp.max(jnp.where(table == expert, 1.0, 0.0), axis=1, keepdims=True)
        named = jnp.where(lane == step, hit, named)
    rank = jnp.dot(earlier, named.astype(BF16), preferred_element_type=F32)
    source = (lax.broadcasted_iota(jnp.int32, (total, LANES), 0) // rows).astype(F32)
    slot = rank + source * capacity
    first = 0
    for out in outs:
        held = out.shape[0]
        stride = out.shape[1] // groups
        place = lax.broadcasted_iota(jnp.int32, out.shape, 1).astype(F32)
        chosen = jnp.zeros(out.shape, F32)
        for step in range(groups):
            at = slot[:held, step : step + 1] - first
            inside = (at >= 0) & (at < stride) & (named[:held, step : step + 1] > 0)
            chosen = jnp.where((place == at + step * stride) & inside, 1.0, chosen)
        out[...] = chosen.astype(BF16)
        first += stride


def pack_kernel(count, *refs):
    blocks, choice, outs = refs[:count], refs[count], refs[count + 2 :]
    stride = outs[0].shape[0]
    packed = lax.dot_general(
        choice[...], stack(blocks).astype(BF16), (((0,), (0,)), ((), ())), preferred_element_type=F32
    )
    for step, out in enumerate(outs):
        out[...] = packed[step * stride : (step + 1) * stride].astype(BF16)


def expert_kernel(groups, *refs):
    blocks, weights, outs = refs[:groups], refs[groups : groups + 6], refs[groups + 6 :]
    stride = outs[0].shape[0]
    inputs = stack(blocks).astype(BF16)
    total = None
    for half in range(2):
        gate, up, down = weights[3 * half : 3 * half + 3]
        gated = jnp.dot(inputs, gate[...], preferred_element_type=F32)
        upper = jnp.dot(inputs, up[...], preferred_element_type=F32)
        active = (gated / (1.0 + jnp.exp(-gated)) * upper).astype(BF16)
        part = jnp.dot(active, down[...], preferred_element_type=F32)
        total = part if total is None else total + part
    for step, out in enumerate(outs):
        out[...] = total[step * stride : (step + 1) * stride].astype(BF16)


def combine_kernel(groups, sets, start, *refs):
    choices, outs = refs[sets * groups : sets * (groups + 1)], refs[sets * (groups + 1) + 1 :]
    rows = outs[0].shape[0]
    summed = None
    for i, choice in enumerate(choices):
        part = jnp.dot(
            choice[start : start + len(outs) * rows],
            stack(refs[i * groups : (i + 1) * groups]).astype(BF16),
            preferred_element_type=F32,
        )
        summed = part if summed is None else summed + part
    for step, out in enumerate(outs):
        out[...] = summed[step * rows : (step + 1) * rows].astype(out.dtype)


def final_kernel(count, picks, *refs):
    blocks, hidden, out = refs[:count], refs[count], refs[count + 1]
    total = blocks[0][...]
    for block in blocks[1:]:
        total = total + block[...].astype(F32)
    out[...] = (hidden[...] + total / picks).astype(BF16)


def body(
    tokens,
    norm_gain,
    q_gain,
    k_gain,
    post_gain,
    w_query,
    w_keyvalue,
    w_out,
    cache_keys,
    cache_values,
    lengths,
    expert_ids,
    w_gate,
    w_up,
    w_down,
):
    count, groups = lax.axis_size("dev"), lax.axis_size("grp")
    rows, width = tokens.shape
    picks = expert_ids.shape[1]
    heads, places, dim = cache_keys.shape[1:]
    query_width, kv_width = w_query.shape[1], w_keyvalue.shape[1]
    group = query_width // dim
    experts = count * groups
    capacity = min(rows, max(3, (rows * picks + experts - 1) // experts + 1))
    strides = [max(8, count // 2 * capacity // 8 * 8)]
    strides.append(max(8, -(-(count * capacity - strides[0]) // 8) * 8))

    half = count // 2
    near, far = list(range(half)), list(range(half, count))
    swap = [(0, 1), (1, 0)]
    own_weights = [w_gate[0], w_up[0], w_down[0]]
    gathered = exchange([tokens] * count, "dev", count)
    other_weights = [lax.ppermute(w, "role", swap) for w in own_weights]
    query_kept, kv_kept, tokens_kept, gain_kept = fetch(w_query, w_keyvalue, tokens, norm_gain.reshape(1, -1))
    gathered[0] = tokens_kept

    chunks = [near] + [[step] for step in far]
    messages = [None] * count
    for chunk in [near, far]:
        made = call(
            functools.partial(project_kernel, len(chunk)),
            [((rows, query_width + kv_width + LANES), BF16)] * len(chunk),
            [VMEM] * (len(chunk) + 4),
            [*[gathered[step] for step in chunk], gain_kept, query_kept, kv_kept, expert_ids.T],
            cost=(2 * len(chunk) * rows * width * (query_width + kv_width), 3 << 20),
            limit=4 << 20,
        )
        if chunk == near:
            lengths, made = lax.optimization_barrier((lengths, made))
        for step, message in zip(chunk, made):
            messages[step] = message
    frequency = rope_base ** (-jnp.arange(dim // 2, dtype=F32) / (dim // 2))
    angles = lengths.astype(F32)[:, None] * frequency[None, :]
    cosine, sine = jnp.cos(angles), jnp.sin(angles)
    cosine = jnp.concatenate([cosine, cosine], axis=1)
    sine = jnp.concatenate([-sine, sine], axis=1)
    visible = jnp.arange(places, dtype=jnp.int32)[None, :] < lengths[:, None]
    bias = jnp.where(visible, 0.0, -jnp.inf).astype(F32)
    messages = exchange(messages, "dev", count)
    parts = []
    gains = [q_gain.reshape(1, -1), k_gain.reshape(1, -1)]
    flops = 4 * rows * group * places * dim
    for chunk in [near]:
        parts += call(
            functools.partial(attend_kernel, chunk),
            [((rows, group, dim), F32)] * (4 * len(chunk)),
            [VMEM] * (len(chunk) + 6) + [ANY],
            [*[messages[step] for step in chunk], gains[0], cosine, sine, bias]
            + [cache_keys, cache_values, parts[-1] if parts else bias],
            scratch=[pltpu.VMEM((len(chunk), rows * group, dim), F32)],
            cost=(len(chunk) * flops, 2 << 20),
            limit=4 << 20,
        )
    mixtures = call(
        functools.partial(mix_kernel, count, half),
        [((rows, query_width), BF16)] * count,
        [VMEM] * (count + 4 * half + 7),
        [*messages, *parts, *gains, cosine, sine, bias, cache_keys, cache_values],
        scratch=[
            pltpu.VMEM((count, rows * group, dim), F32),
            pltpu.VMEM((heads, rows, dim), F32),
            pltpu.VMEM((heads, rows, dim), F32),
            pltpu.VMEM((count, rows, kv_width), F32),
        ],
        cost=(flops, 2 << 20),
        limit=4 << 20,
    )
    choices = call(
        functools.partial(route_kernel, count, groups, capacity),
        [((half * rows, groups * strides[0]), BF16), ((count * rows, groups * strides[1]), BF16)],
        [VMEM] * count,
        [*messages],
        cost=(0, 2 << 20),
        limit=2 << 20,
    )
    mixtures = exchange(mixtures, "dev", count)
    partials = [None] * count
    for chunk in chunks:
        made = call(
            functools.partial(out_kernel, len(chunk)),
            [((rows, width), BF16 if step else F32) for step in chunk],
            [VMEM] * (len(chunk) + 1),
            [*[mixtures[step] for step in chunk], w_out],
            cost=(2 * len(chunk) * rows * width * query_width, 2 << 20),
            limit=4 << 20,
        )
        for step, partial in zip(chunk, made):
            partials[step] = partial
    partials = exchange(partials, "dev", count)
    hidden, ready = call(
        functools.partial(ready_kernel, count),
        [((rows, width), F32), ((rows, width), BF16)],
        [VMEM] * (count + 2),
        [*partials, tokens_kept, post_gain.reshape(1, -1)],
        cost=(0, 1 << 20),
        limit=8 << 20,
    )
    ready = exchange([ready] * count, "dev", count)
    results = []
    after = hidden
    for part, choice, stride in zip((near, near + far), choices, strides):
        packed = call(
            functools.partial(pack_kernel, len(part)),
            [((stride, width), BF16)] * groups,
            [VMEM] * (len(part) + 1) + [ANY],
            [*[ready[step] for step in part], choice, after],
            cost=(0, 1 << 20),
            limit=4 << 20,
        )
        after = packed[0]
        packed = exchange(packed, "grp", groups)
        results.append(
            call(
                functools.partial(expert_kernel, groups),
                [((stride, width), BF16)] * groups,
                [VMEM] * (groups + 6),
                [*packed, *own_weights, *other_weights],
                cost=(6 * groups * stride * width * w_gate.shape[2] * 2, 4 << 20),
                limit=8 << 20,
            )
        )
    results = lax.optimization_barrier(results)
    sums = [None] * count
    after = hidden
    held = [None, exchange(results[1], "grp", groups)]
    held[0] = exchange(results[0], "grp", groups)
    for part, used in ((far, [1]), (near, [0, 1])):
        made = call(
            functools.partial(combine_kernel, groups, len(used), part[0] * rows),
            [((rows, width), BF16 if step else F32) for step in part],
            [VMEM] * (len(used) * (groups + 1)) + [ANY],
            [*sum([held[i] for i in used], []), *[choices[i] for i in used], after],
            cost=(0, 1 << 20),
            limit=4 << 20,
        )
        after = made[0]
        for step, total in zip(part, made):
            sums[step] = total
    sums = exchange(sums, "dev", count)
    [output] = call(
        functools.partial(final_kernel, count, picks),
        [((rows, width), BF16)],
        [VMEM] * (count + 1),
        [*sums, hidden],
        cost=(0, 1 << 20),
        limit=8 << 20,
        kept=False,
    )
    return output


def rms_scale(values, gain):
    widened = values.astype(jnp.float32)
    mean_square = jnp.mean(widened * widened, axis=-1, keepdims=True)
    return widened * lax.rsqrt(mean_square + epsilon) * gain


def rotate(values, positions):
    half_dim = values.shape[-1] // 2
    frequency = rope_base ** (-jnp.arange(half_dim, dtype=jnp.float32) / half_dim)
    angles = positions.astype(jnp.float32)[:, None, None] * frequency[None, None, :]
    cosine = jnp.cos(angles)
    sine_part = jnp.sin(angles)
    first_half = values[..., :half_dim]
    second_half = values[..., half_dim:]
    return jnp.concatenate(
        [
            first_half * cosine - second_half * sine_part,
            second_half * cosine + first_half * sine_part,
        ],
        axis=-1,
    )


def attend(queries, fresh_kv, cache_keys, cache_values, lengths, q_gain, k_gain):
    batch_rows = queries.shape[0]
    kv_heads = cache_keys.shape[1]
    cache_len = cache_keys.shape[2]
    head_dim = cache_keys.shape[3]
    head_count = queries.shape[1] // head_dim
    group_size = head_count // kv_heads
    scaled_q = rotate(
        rms_scale(queries.reshape(batch_rows, head_count, head_dim), q_gain), lengths
    ).astype(jnp.bfloat16)
    fresh_keys = fresh_kv[:, : kv_heads * head_dim].reshape(batch_rows, kv_heads, head_dim)
    fresh_values = fresh_kv[:, kv_heads * head_dim :].reshape(batch_rows, kv_heads, head_dim)
    scaled_k = rotate(rms_scale(fresh_keys, k_gain), lengths).astype(jnp.bfloat16)
    grouped = scaled_q.reshape(batch_rows, kv_heads, group_size, head_dim)
    factor = head_dim ** (-0.5)
    old_scores = (
        jnp.einsum("rgqd,rgkd->rgqk", grouped, cache_keys, preferred_element_type=jnp.float32)
        * factor
    )
    new_scores = (
        jnp.einsum("rgqd,rgd->rgq", grouped, scaled_k, preferred_element_type=jnp.float32) * factor
    )
    visible = jnp.arange(cache_len, dtype=jnp.int32)[None, :] < lengths[:, None]
    old_scores = jnp.where(visible[:, None, None, :], old_scores, -jnp.inf)
    highest = jnp.maximum(jnp.max(old_scores, axis=-1), new_scores)
    old_weights = jnp.exp(old_scores - highest[..., None])
    new_weights = jnp.exp(new_scores - highest)
    denominator = jnp.sum(old_weights, axis=-1) + new_weights
    old_weights = (old_weights / denominator[..., None]).astype(jnp.bfloat16)
    new_weights = (new_weights / denominator).astype(jnp.bfloat16)
    mixture = jnp.einsum(
        "rgqk,rgkd->rgqd", old_weights, cache_values, preferred_element_type=jnp.float32
    )
    mixture = (
        mixture
        + new_weights.astype(jnp.float32)[..., None]
        * fresh_values.astype(jnp.float32)[:, :, None, :]
    )
    return mixture.reshape(batch_rows, head_count * head_dim).astype(jnp.bfloat16)


def expert_rows(inputs, gate_w, up_w, down_w):
    gate_part = jnp.dot(inputs, gate_w, preferred_element_type=jnp.float32)
    upper_part = jnp.dot(inputs, up_w, preferred_element_type=jnp.float32)
    activated = (jax.nn.silu(gate_part) * upper_part).astype(jnp.bfloat16)
    return jnp.dot(activated, down_w, preferred_element_type=jnp.float32)


def general_body(
    tokens,
    norm_gain,
    q_gain,
    k_gain,
    post_gain,
    w_query,
    w_keyvalue,
    w_out,
    cache_keys,
    cache_values,
    lengths,
    expert_ids,
    w_gate,
    w_up,
    w_down,
):
    normed = rms_scale(tokens, norm_gain).astype(jnp.bfloat16)
    query_width = w_query.shape[1]
    piece = lax.all_gather(normed, "dev", axis=0, tiled=True)
    joined = jnp.concatenate(
        [
            jnp.dot(piece, w_query, preferred_element_type=jnp.float32),
            jnp.dot(piece, w_keyvalue, preferred_element_type=jnp.float32),
        ],
        axis=1,
    )
    projected = joined.astype(jnp.bfloat16)
    queries, fresh_kv = (
        lax.all_to_all(projected[:, :query_width], "dev", split_axis=0, concat_axis=1, tiled=True),
        lax.all_to_all(projected[:, query_width:], "dev", split_axis=0, concat_axis=1, tiled=True),
    )
    mixture = attend(queries, fresh_kv, cache_keys, cache_values, lengths, q_gain, k_gain)
    head_rows = lax.all_to_all(mixture, "dev", split_axis=1, concat_axis=0, tiled=True)
    own_rows = tokens.shape[0]
    attended = lax.psum_scatter(
        jnp.dot(head_rows, w_out, preferred_element_type=jnp.float32).astype(jnp.bfloat16),
        "dev",
        scatter_dimension=0,
        tiled=True,
    ).astype(jnp.float32)
    hidden = tokens.astype(jnp.float32) + attended
    ready = rms_scale(hidden, post_gain).astype(jnp.bfloat16)
    picks = expert_ids.shape[1]
    group_count = lax.axis_size("grp")
    member_count = lax.axis_size("dev")
    expert_count = group_count * member_count
    capacity = min(own_rows, max(3, (own_rows * picks + expert_count - 1) // expert_count + 1))
    model_width = tokens.shape[1]
    flat_ids = expert_ids.reshape(own_rows * picks)
    order_index = jnp.arange(own_rows * picks, dtype=jnp.int32)
    earlier = (flat_ids[:, None] == flat_ids[None, :]) & (
        order_index[None, :] < order_index[:, None]
    )
    slot_index = jnp.sum(earlier.astype(jnp.int32), axis=1)
    position = (flat_ids * capacity + slot_index).reshape(own_rows, picks)
    buffer_rows = jnp.arange(expert_count * capacity, dtype=jnp.int32)
    placing = jnp.any(position[None, :, :] == buffer_rows[:, None, None], axis=2).astype(
        jnp.bfloat16
    )
    outgoing = jnp.dot(placing, ready, preferred_element_type=jnp.float32).astype(jnp.bfloat16)
    arrived = lax.all_to_all(
        outgoing.reshape(expert_count, capacity, model_width),
        ("grp", "dev"),
        split_axis=0,
        concat_axis=0,
        tiled=True,
    )
    arrived = arrived.reshape(expert_count * capacity, model_width)
    full_gate, full_up, full_down = (
        lax.all_gather(w_gate, "role", axis=2, tiled=True),
        lax.all_gather(w_up, "role", axis=2, tiled=True),
        lax.all_gather(w_down, "role", axis=1, tiled=True),
    )
    expert_out = expert_rows(arrived, full_gate[0], full_up[0], full_down[0]).astype(jnp.bfloat16)
    returned = lax.all_to_all(
        expert_out.reshape(expert_count, capacity, model_width),
        ("grp", "dev"),
        split_axis=0,
        concat_axis=0,
        tiled=True,
    )
    returned = returned.reshape(expert_count * capacity, model_width)
    selected = (
        jnp.take(returned, position.reshape(own_rows * picks), axis=0)
        .astype(jnp.float32)
        .reshape(own_rows, picks, model_width)
    )
    output = hidden + jnp.sum(selected, axis=1) / picks
    return output.astype(jnp.bfloat16)


def solution(mesh):
    sizes = dict(mesh.shape)

    def step(*args):
        heads = args[8].shape[1]
        powers = all(sizes[axis] & (sizes[axis] - 1) == 0 for axis in ("grp", "dev"))
        fitted = sizes["dev"] == heads and sizes["role"] == 2 and powers
        if not fitted:
            return general_body(*args)
        return body(*args)

    return jax.shard_map(
        step,
        mesh=mesh,
        in_specs=(
            P(("role", "grp", "dev"), None),
            P(),
            P(),
            P(),
            P(),
            P(None, "dev"),
            P(None, "dev"),
            P("dev", None),
            P(("role", "grp", "dev"), None, None, None),
            P(("role", "grp", "dev"), None, None, None),
            P(("role", "grp", "dev")),
            P(("role", "grp", "dev"), None),
            P(("grp", "dev"), None, "role"),
            P(("grp", "dev"), None, "role"),
            P(("grp", "dev"), "role", None),
        ),
        out_specs=P(("role", "grp", "dev"), None),
        check_vma=False,
    )
```

```python
import functools

import jax
import jax.numpy as jnp
from jax import lax
from jax.experimental import pallas as pl
from jax.experimental.pallas import tpu as pltpu
from jax.sharding import PartitionSpec as P


epsilon = 1e-06
rope_base = 1000000.0
LANES = 128
VMEM = pl.BlockSpec(memory_space=pltpu.VMEM)
ANY = pl.BlockSpec(memory_space=pl.ANY)
F32 = jnp.float32
BF16 = jnp.bfloat16


def call(kernel, outs, specs, args, scratch=(), cost=None, limit=None, kept=True):
    flops, moved = cost or (0, 0)
    place = pltpu.VMEM if kept else jax.ShapeDtypeStruct
    return pl.pallas_call(
        kernel,
        out_shape=[place(shape, dtype) for shape, dtype in outs],
        in_specs=list(specs),
        out_specs=[VMEM] * len(outs),
        scratch_shapes=list(scratch),
        cost_estimate=pl.CostEstimate(flops=flops, bytes_accessed=moved, transcendentals=0),
        compiler_params=pltpu.CompilerParams(vmem_limit_bytes=limit),
    )(*args)


def exchange(pieces, axis, size):
    got = [pieces[0]]
    for step in range(1, size):
        got.append(lax.ppermute(pieces[step], axis, [(i, i ^ step) for i in range(size)]))
    return got


def fetch_kernel(count, *refs):
    sources, targets, sems = refs[:count], refs[count : 2 * count], refs[2 * count]
    copies = [pltpu.make_async_copy(a, b, sems.at[i]) for i, (a, b) in enumerate(zip(sources, targets))]
    for copy in copies:
        copy.start()
    for copy in copies:
        copy.wait()


def fetch(*arrays, held=True):
    moved = sum(a.size * a.dtype.itemsize for a in arrays)
    return call(
        functools.partial(fetch_kernel, len(arrays)),
        [(a.shape, a.dtype) for a in arrays],
        [ANY] * len(arrays),
        [pltpu.with_memory_space_constraint(a, pltpu.HBM) if held else a for a in arrays],
        scratch=[pltpu.SemaphoreType.DMA((len(arrays),))],
        cost=(0, moved),
        limit=1 << 20,
    )


def rms(values, gain):
    mean_square = jnp.mean(values * values, axis=-1, keepdims=True)
    return values * lax.rsqrt(mean_square + epsilon) * gain


def stack(refs):
    return jnp.concatenate([ref[...].astype(F32) for ref in refs], axis=0)


def project_kernel(count, *refs):
    blocks, (gain, w_query, w_keyvalue, ids), outs = refs[:count], refs[count : count + 4], refs[count + 4 :]
    rows = blocks[0].shape[0]
    query_width = w_query.shape[1]
    kv_width = w_keyvalue.shape[1]
    picks = ids.shape[0]
    spread = lax.broadcasted_iota(jnp.int32, (picks, LANES), 0) == lax.broadcasted_iota(jnp.int32, (picks, LANES), 1)
    named = lax.dot_general(
        ids[...].astype(F32).astype(BF16),
        jnp.where(spread, 1.0, 0.0).astype(BF16),
        (((0,), (0,)), ((), ())),
        preferred_element_type=F32,
    )
    lane = lax.broadcasted_iota(jnp.int32, named.shape, 1)
    named = jnp.where(lane < picks, named, -1.0).astype(BF16)
    normed = rms(stack(blocks), gain[...]).astype(BF16)
    queries = jnp.dot(normed, w_query[...], preferred_element_type=F32)
    fresh = jnp.dot(normed, w_keyvalue[...], preferred_element_type=F32)
    for step in range(count):
        own = slice(step * rows, (step + 1) * rows)
        outs[step][:, :query_width] = queries[own].astype(BF16)
        outs[step][:, query_width : query_width + kv_width] = fresh[own].astype(BF16)
        outs[step][:, query_width + kv_width :] = named


def turn(values, gain, cosine, sine):
    values = rms(values, gain)
    return values * cosine + pltpu.roll(values, values.shape[1] // 2, 1) * sine


def attend_cache(message, head, gain, cosine, sine, bias, keys, values, scratch):
    rows, _, _, dim = keys.shape
    group = scratch.shape[0] // rows
    for h in range(group):
        piece = message[:, h * dim : (h + 1) * dim].astype(F32)
        scratch[pl.ds(h, rows, stride=group), :] = turn(piece, gain, cosine, sine)
    query = scratch[...].reshape(rows, group, dim).astype(BF16)
    scores = jnp.einsum("rqd,rkd->rqk", query, keys[:, head], preferred_element_type=F32) * dim ** (-0.5)
    scores = scores + bias[:, None, :]
    top = jnp.max(scores, axis=-1, keepdims=True)
    weights = jnp.exp(scores - top)
    total = jnp.sum(weights, axis=-1, keepdims=True)
    mixed = jnp.einsum("rqk,rkd->rqd", weights.astype(BF16), values[:, head], preferred_element_type=F32)
    return query.astype(F32), top, total, mixed


def attend_kernel(steps, *refs):
    count = len(steps)
    me = lax.axis_index("dev")
    messages = refs[:count]
    gain, cosine, sine, bias, keys, values = refs[count : count + 6]
    outs, scratch = refs[count + 7 : -1], refs[-1]
    for i, step in enumerate(steps):
        found = attend_cache(
            messages[i], me ^ step, gain[...], cosine[...], sine[...], bias[...], keys, values, scratch.at[i]
        )
        for out, value in zip(outs[4 * i : 4 * i + 4], found):
            out[...] = jnp.broadcast_to(value, out.shape)


def mix_kernel(count, done, *refs):
    messages, parts = refs[:count], refs[count : count + 4 * done]
    refs = refs[count + 4 * done :]
    q_gain, k_gain, cosine, sine, bias, keys, values = refs[:7]
    outs = refs[7 : 7 + count]
    scratch, k_rot, v_new, kv_all = refs[7 + count :]
    me = lax.axis_index("dev")
    rows, heads, _, dim = keys.shape
    group = scratch.shape[1] // rows
    query_width = group * dim
    kv_width = kv_all.shape[2]
    cos, sin = cosine[...], sine[...]
    last = [
        attend_cache(messages[step], me ^ step, q_gain[...], cos, sin, bias[...], keys, values, scratch.at[step])
        for step in range(done, count)
    ]
    for step in range(count):
        kv_all[me ^ step] = messages[step][:, query_width : query_width + kv_width].astype(F32)
    for h in range(2 * heads):
        column = h * dim
        piece = kv_all[column // kv_width, :, column % kv_width : column % kv_width + dim]
        if h < heads:
            k_rot[h] = turn(piece, k_gain[...], cos, sin).astype(BF16).astype(F32)
        else:
            v_new[h - heads] = piece
    for step in reversed(range(count)):
        head = me ^ step
        if step < done:
            query, top, total, mixed = [ref[...] for ref in parts[4 * step : 4 * step + 4]]
            top, total = top[:, :, :1], total[:, :, :1]
        else:
            query, top, total, mixed = last[step - done]
        new = jnp.sum(query * k_rot[head][:, None, :], axis=-1, keepdims=True) * dim ** (-0.5)
        highest = jnp.maximum(top, new)
        old = jnp.exp(top - highest)
        new = jnp.exp(new - highest)
        share = 1.0 / (total * old + new)
        out = mixed * (old * share) + (new * share) * v_new[head][:, None, :]
        scratch[step] = out.reshape(rows * group, dim)
        for h in range(group):
            outs[step][:, h * dim : (h + 1) * dim] = scratch[step, pl.ds(h, rows, stride=group), :].astype(BF16)


def out_kernel(count, *refs):
    blocks, w_out, outs = refs[:count], refs[count], refs[count + 1 :]
    rows = blocks[0].shape[0]
    partial = jnp.dot(stack(blocks).astype(BF16), w_out[...], preferred_element_type=F32)
    for step in range(count):
        outs[step][...] = partial[step * rows : (step + 1) * rows].astype(outs[step].dtype)


def ready_kernel(count, *refs):
    blocks, (tokens, gain), (hidden, ready) = refs[:count], refs[count : count + 2], refs[count + 2 :]
    total = blocks[0][...]
    for block in blocks[1:]:
        total = total + block[...].astype(F32)
    total = tokens[...].astype(F32) + total
    hidden[...] = total
    ready[...] = rms(total, gain[...]).astype(BF16)


def route_kernel(count, groups, capacity, *refs):
    messages, outs = refs[:count], refs[count:]
    dev, grp = lax.axis_index("dev"), lax.axis_index("grp")
    rows, columns = messages[0].shape
    total = count * rows
    lane = lax.broadcasted_iota(jnp.int32, (total, LANES), 1)
    down = lax.broadcasted_iota(jnp.int32, (total, total), 0)
    across = lax.broadcasted_iota(jnp.int32, (total, total), 1)
    earlier = jnp.where((across < down) & (across // rows == down // rows), 1.0, 0.0).astype(BF16)
    table = jnp.concatenate([m[:, columns - LANES :].astype(F32) for m in messages], axis=0)
    named = jnp.zeros((total, LANES), F32)
    for step in range(groups):
        expert = ((grp ^ step) * count + dev).astype(F32)
        hit = jnp.max(jnp.where(table == expert, 1.0, 0.0), axis=1, keepdims=True)
        named = jnp.where(lane == step, hit, named)
    rank = jnp.dot(earlier, named.astype(BF16), preferred_element_type=F32)
    source = (lax.broadcasted_iota(jnp.int32, (total, LANES), 0) // rows).astype(F32)
    slot = rank + source * capacity
    first = 0
    for out in outs:
        held = out.shape[0]
        stride = out.shape[1] // groups
        place = lax.broadcasted_iota(jnp.int32, out.shape, 1).astype(F32)
        chosen = jnp.zeros(out.shape, F32)
        for step in range(groups):
            at = slot[:held, step : step + 1] - first
            inside = (at >= 0) & (at < stride) & (named[:held, step : step + 1] > 0)
            chosen = jnp.where((place == at + step * stride) & inside, 1.0, chosen)
        out[...] = chosen.astype(BF16)
        first += stride


def pack_kernel(count, *refs):
    blocks, choice, outs = refs[:count], refs[count], refs[count + 2 :]
    stride = outs[0].shape[0]
    packed = lax.dot_general(
        choice[...], stack(blocks).astype(BF16), (((0,), (0,)), ((), ())), preferred_element_type=F32
    )
    for step, out in enumerate(outs):
        out[...] = packed[step * stride : (step + 1) * stride].astype(BF16)


def expert_kernel(groups, *refs):
    blocks, weights, outs = refs[:groups], refs[groups : groups + 6], refs[groups + 6 :]
    stride = outs[0].shape[0]
    inputs = stack(blocks).astype(BF16)
    total = None
    for half in range(2):
        gate, up, down = weights[3 * half : 3 * half + 3]
        gated = jnp.dot(inputs, gate[...], preferred_element_type=F32)
        upper = jnp.dot(inputs, up[...], preferred_element_type=F32)
        active = (gated / (1.0 + jnp.exp(-gated)) * upper).astype(BF16)
        part = jnp.dot(active, down[...], preferred_element_type=F32)
        total = part if total is None else total + part
    for step, out in enumerate(outs):
        out[...] = total[step * stride : (step + 1) * stride].astype(BF16)


def combine_kernel(groups, sets, start, *refs):
    choices, outs = refs[sets * groups : sets * (groups + 1)], refs[sets * (groups + 1) + 1 :]
    rows = outs[0].shape[0]
    summed = None
    for i, choice in enumerate(choices):
        part = jnp.dot(
            choice[start : start + len(outs) * rows],
            stack(refs[i * groups : (i + 1) * groups]).astype(BF16),
            preferred_element_type=F32,
        )
        summed = part if summed is None else summed + part
    for step, out in enumerate(outs):
        out[...] = summed[step * rows : (step + 1) * rows].astype(out.dtype)


def final_kernel(count, picks, *refs):
    blocks, hidden, out = refs[:count], refs[count], refs[count + 1]
    total = blocks[0][...]
    for block in blocks[1:]:
        total = total + block[...].astype(F32)
    out[...] = (hidden[...] + total / picks).astype(BF16)


def body(
    tokens,
    norm_gain,
    q_gain,
    k_gain,
    post_gain,
    w_query,
    w_keyvalue,
    w_out,
    cache_keys,
    cache_values,
    lengths,
    expert_ids,
    w_gate,
    w_up,
    w_down,
):
    count, groups = lax.axis_size("dev"), lax.axis_size("grp")
    rows, width = tokens.shape
    picks = expert_ids.shape[1]
    heads, places, dim = cache_keys.shape[1:]
    query_width, kv_width = w_query.shape[1], w_keyvalue.shape[1]
    group = query_width // dim
    experts = count * groups
    capacity = min(rows, max(3, (rows * picks + experts - 1) // experts + 1))
    strides = [max(8, count // 2 * capacity // 8 * 8)]
    strides.append(max(8, -(-(count * capacity - strides[0]) // 8) * 8))

    half = count // 2
    near, far = list(range(half)), list(range(half, count))
    swap = [(0, 1), (1, 0)]
    own_weights = [w_gate[0], w_up[0], w_down[0]]
    gathered = exchange([tokens] * count, "dev", count)
    other_weights = [lax.ppermute(w, "role", swap) for w in own_weights]
    query_kept, kv_kept, tokens_kept, gain_kept = fetch(w_query, w_keyvalue, tokens, norm_gain.reshape(1, -1))
    gathered[0] = tokens_kept

    chunks = [near] + [[step] for step in far]
    messages = [None] * count
    for chunk in [near, far]:
        made = call(
            functools.partial(project_kernel, len(chunk)),
            [((rows, query_width + kv_width + LANES), BF16)] * len(chunk),
            [VMEM] * (len(chunk) + 4),
            [*[gathered[step] for step in chunk], gain_kept, query_kept, kv_kept, expert_ids.T],
            cost=(2 * len(chunk) * rows * width * (query_width + kv_width), 3 << 20),
            limit=4 << 20,
        )
        if chunk == near:
            lengths, made = lax.optimization_barrier((lengths, made))
        for step, message in zip(chunk, made):
            messages[step] = message
    frequency = rope_base ** (-jnp.arange(dim // 2, dtype=F32) / (dim // 2))
    angles = lengths.astype(F32)[:, None] * frequency[None, :]
    cosine, sine = jnp.cos(angles), jnp.sin(angles)
    cosine = jnp.concatenate([cosine, cosine], axis=1)
    sine = jnp.concatenate([-sine, sine], axis=1)
    visible = jnp.arange(places, dtype=jnp.int32)[None, :] < lengths[:, None]
    bias = jnp.where(visible, 0.0, -jnp.inf).astype(F32)
    messages = exchange(messages, "dev", count)
    parts = []
    gains = [q_gain.reshape(1, -1), k_gain.reshape(1, -1)]
    flops = 4 * rows * group * places * dim
    for chunk in chunks[:-1]:
        parts += call(
            functools.partial(attend_kernel, chunk),
            [((rows, group, dim), F32)] * (4 * len(chunk)),
            [VMEM] * (len(chunk) + 6) + [ANY],
            [*[messages[step] for step in chunk], gains[0], cosine, sine, bias]
            + [cache_keys, cache_values, parts[-1] if parts else bias],
            scratch=[pltpu.VMEM((len(chunk), rows * group, dim), F32)],
            cost=(len(chunk) * flops, 2 << 20),
            limit=4 << 20,
        )
    mixtures = call(
        functools.partial(mix_kernel, count, count - 1),
        [((rows, query_width), BF16)] * count,
        [VMEM] * (count + 4 * (count - 1) + 7),
        [*messages, *parts, *gains, cosine, sine, bias, cache_keys, cache_values],
        scratch=[
            pltpu.VMEM((count, rows * group, dim), F32),
            pltpu.VMEM((heads, rows, dim), F32),
            pltpu.VMEM((heads, rows, dim), F32),
            pltpu.VMEM((count, rows, kv_width), F32),
        ],
        cost=(flops, 2 << 20),
        limit=4 << 20,
    )
    choices = call(
        functools.partial(route_kernel, count, groups, capacity),
        [((half * rows, groups * strides[0]), BF16), ((count * rows, groups * strides[1]), BF16)],
        [VMEM] * count,
        [*messages],
        cost=(0, 2 << 20),
        limit=2 << 20,
    )
    mixtures = exchange(mixtures, "dev", count)
    partials = [None] * count
    for chunk in chunks:
        made = call(
            functools.partial(out_kernel, len(chunk)),
            [((rows, width), BF16 if step else F32) for step in chunk],
            [VMEM] * (len(chunk) + 1),
            [*[mixtures[step] for step in chunk], w_out],
            cost=(2 * len(chunk) * rows * width * query_width, 2 << 20),
            limit=4 << 20,
        )
        for step, partial in zip(chunk, made):
            partials[step] = partial
    partials = exchange(partials, "dev", count)
    hidden, ready = call(
        functools.partial(ready_kernel, count),
        [((rows, width), F32), ((rows, width), BF16)],
        [VMEM] * (count + 2),
        [*partials, tokens_kept, post_gain.reshape(1, -1)],
        cost=(0, 1 << 20),
        limit=8 << 20,
    )
    ready = exchange([ready] * count, "dev", count)
    results = []
    after = hidden
    for part, choice, stride in zip((near, near + far), choices, strides):
        packed = call(
            functools.partial(pack_kernel, len(part)),
            [((stride, width), BF16)] * groups,
            [VMEM] * (len(part) + 1) + [ANY],
            [*[ready[step] for step in part], choice, after],
            cost=(0, 1 << 20),
            limit=4 << 20,
        )
        after = packed[0]
        packed = exchange(packed, "grp", groups)
        results.append(
            call(
                functools.partial(expert_kernel, groups),
                [((stride, width), BF16)] * groups,
                [VMEM] * (groups + 6),
                [*packed, *own_weights, *other_weights],
                cost=(6 * groups * stride * width * w_gate.shape[2] * 2, 4 << 20),
                limit=8 << 20,
            )
        )
    sums = [None] * count
    after = hidden
    held = [None, exchange(results[1], "grp", groups)]
    held[0] = exchange(results[0], "grp", groups)
    for part, used in ((far, [1]), (near, [0, 1])):
        made = call(
            functools.partial(combine_kernel, groups, len(used), part[0] * rows),
            [((rows, width), BF16 if step else F32) for step in part],
            [VMEM] * (len(used) * (groups + 1)) + [ANY],
            [*sum([held[i] for i in used], []), *[choices[i] for i in used], after],
            cost=(0, 1 << 20),
            limit=4 << 20,
        )
        after = made[0]
        for step, total in zip(part, made):
            sums[step] = total
    sums = exchange(sums, "dev", count)
    [output] = call(
        functools.partial(final_kernel, count, picks),
        [((rows, width), BF16)],
        [VMEM] * (count + 1),
        [*sums, hidden],
        cost=(0, 1 << 20),
        limit=8 << 20,
        kept=False,
    )
    return output


def rms_scale(values, gain):
    widened = values.astype(jnp.float32)
    mean_square = jnp.mean(widened * widened, axis=-1, keepdims=True)
    return widened * lax.rsqrt(mean_square + epsilon) * gain


def rotate(values, positions):
    half_dim = values.shape[-1] // 2
    frequency = rope_base ** (-jnp.arange(half_dim, dtype=jnp.float32) / half_dim)
    angles = positions.astype(jnp.float32)[:, None, None] * frequency[None, None, :]
    cosine = jnp.cos(angles)
    sine_part = jnp.sin(angles)
    first_half = values[..., :half_dim]
    second_half = values[..., half_dim:]
    return jnp.concatenate(
        [
            first_half * cosine - second_half * sine_part,
            second_half * cosine + first_half * sine_part,
        ],
        axis=-1,
    )


def attend(queries, fresh_kv, cache_keys, cache_values, lengths, q_gain, k_gain):
    batch_rows = queries.shape[0]
    kv_heads = cache_keys.shape[1]
    cache_len = cache_keys.shape[2]
    head_dim = cache_keys.shape[3]
    head_count = queries.shape[1] // head_dim
    group_size = head_count // kv_heads
    scaled_q = rotate(
        rms_scale(queries.reshape(batch_rows, head_count, head_dim), q_gain), lengths
    ).astype(jnp.bfloat16)
    fresh_keys = fresh_kv[:, : kv_heads * head_dim].reshape(batch_rows, kv_heads, head_dim)
    fresh_values = fresh_kv[:, kv_heads * head_dim :].reshape(batch_rows, kv_heads, head_dim)
    scaled_k = rotate(rms_scale(fresh_keys, k_gain), lengths).astype(jnp.bfloat16)
    grouped = scaled_q.reshape(batch_rows, kv_heads, group_size, head_dim)
    factor = head_dim ** (-0.5)
    old_scores = (
        jnp.einsum("rgqd,rgkd->rgqk", grouped, cache_keys, preferred_element_type=jnp.float32)
        * factor
    )
    new_scores = (
        jnp.einsum("rgqd,rgd->rgq", grouped, scaled_k, preferred_element_type=jnp.float32) * factor
    )
    visible = jnp.arange(cache_len, dtype=jnp.int32)[None, :] < lengths[:, None]
    old_scores = jnp.where(visible[:, None, None, :], old_scores, -jnp.inf)
    highest = jnp.maximum(jnp.max(old_scores, axis=-1), new_scores)
    old_weights = jnp.exp(old_scores - highest[..., None])
    new_weights = jnp.exp(new_scores - highest)
    denominator = jnp.sum(old_weights, axis=-1) + new_weights
    old_weights = (old_weights / denominator[..., None]).astype(jnp.bfloat16)
    new_weights = (new_weights / denominator).astype(jnp.bfloat16)
    mixture = jnp.einsum(
        "rgqk,rgkd->rgqd", old_weights, cache_values, preferred_element_type=jnp.float32
    )
    mixture = (
        mixture
        + new_weights.astype(jnp.float32)[..., None]
        * fresh_values.astype(jnp.float32)[:, :, None, :]
    )
    return mixture.reshape(batch_rows, head_count * head_dim).astype(jnp.bfloat16)


def expert_rows(inputs, gate_w, up_w, down_w):
    gate_part = jnp.dot(inputs, gate_w, preferred_element_type=jnp.float32)
    upper_part = jnp.dot(inputs, up_w, preferred_element_type=jnp.float32)
    activated = (jax.nn.silu(gate_part) * upper_part).astype(jnp.bfloat16)
    return jnp.dot(activated, down_w, preferred_element_type=jnp.float32)


def general_body(
    tokens,
    norm_gain,
    q_gain,
    k_gain,
    post_gain,
    w_query,
    w_keyvalue,
    w_out,
    cache_keys,
    cache_values,
    lengths,
    expert_ids,
    w_gate,
    w_up,
    w_down,
):
    normed = rms_scale(tokens, norm_gain).astype(jnp.bfloat16)
    query_width = w_query.shape[1]
    piece = lax.all_gather(normed, "dev", axis=0, tiled=True)
    joined = jnp.concatenate(
        [
            jnp.dot(piece, w_query, preferred_element_type=jnp.float32),
            jnp.dot(piece, w_keyvalue, preferred_element_type=jnp.float32),
        ],
        axis=1,
    )
    projected = joined.astype(jnp.bfloat16)
    queries, fresh_kv = (
        lax.all_to_all(projected[:, :query_width], "dev", split_axis=0, concat_axis=1, tiled=True),
        lax.all_to_all(projected[:, query_width:], "dev", split_axis=0, concat_axis=1, tiled=True),
    )
    mixture = attend(queries, fresh_kv, cache_keys, cache_values, lengths, q_gain, k_gain)
    head_rows = lax.all_to_all(mixture, "dev", split_axis=1, concat_axis=0, tiled=True)
    own_rows = tokens.shape[0]
    attended = lax.psum_scatter(
        jnp.dot(head_rows, w_out, preferred_element_type=jnp.float32).astype(jnp.bfloat16),
        "dev",
        scatter_dimension=0,
        tiled=True,
    ).astype(jnp.float32)
    hidden = tokens.astype(jnp.float32) + attended
    ready = rms_scale(hidden, post_gain).astype(jnp.bfloat16)
    picks = expert_ids.shape[1]
    group_count = lax.axis_size("grp")
    member_count = lax.axis_size("dev")
    expert_count = group_count * member_count
    capacity = min(own_rows, max(3, (own_rows * picks + expert_count - 1) // expert_count + 1))
    model_width = tokens.shape[1]
    flat_ids = expert_ids.reshape(own_rows * picks)
    order_index = jnp.arange(own_rows * picks, dtype=jnp.int32)
    earlier = (flat_ids[:, None] == flat_ids[None, :]) & (
        order_index[None, :] < order_index[:, None]
    )
    slot_index = jnp.sum(earlier.astype(jnp.int32), axis=1)
    position = (flat_ids * capacity + slot_index).reshape(own_rows, picks)
    buffer_rows = jnp.arange(expert_count * capacity, dtype=jnp.int32)
    placing = jnp.any(position[None, :, :] == buffer_rows[:, None, None], axis=2).astype(
        jnp.bfloat16
    )
    outgoing = jnp.dot(placing, ready, preferred_element_type=jnp.float32).astype(jnp.bfloat16)
    arrived = lax.all_to_all(
        outgoing.reshape(expert_count, capacity, model_width),
        ("grp", "dev"),
        split_axis=0,
        concat_axis=0,
        tiled=True,
    )
    arrived = arrived.reshape(expert_count * capacity, model_width)
    full_gate, full_up, full_down = (
        lax.all_gather(w_gate, "role", axis=2, tiled=True),
        lax.all_gather(w_up, "role", axis=2, tiled=True),
        lax.all_gather(w_down, "role", axis=1, tiled=True),
    )
    expert_out = expert_rows(arrived, full_gate[0], full_up[0], full_down[0]).astype(jnp.bfloat16)
    returned = lax.all_to_all(
        expert_out.reshape(expert_count, capacity, model_width),
        ("grp", "dev"),
        split_axis=0,
        concat_axis=0,
        tiled=True,
    )
    returned = returned.reshape(expert_count * capacity, model_width)
    selected = (
        jnp.take(returned, position.reshape(own_rows * picks), axis=0)
        .astype(jnp.float32)
        .reshape(own_rows, picks, model_width)
    )
    output = hidden + jnp.sum(selected, axis=1) / picks
    return output.astype(jnp.bfloat16)


def solution(mesh):
    sizes = dict(mesh.shape)

    def step(*args):
        heads = args[8].shape[1]
        powers = all(sizes[axis] & (sizes[axis] - 1) == 0 for axis in ("grp", "dev"))
        fitted = sizes["dev"] == heads and sizes["role"] == 2 and powers
        if not fitted:
            return general_body(*args)
        return body(*args)

    return jax.shard_map(
        step,
        mesh=mesh,
        in_specs=(
            P(("role", "grp", "dev"), None),
            P(),
            P(),
            P(),
            P(),
            P(None, "dev"),
            P(None, "dev"),
            P("dev", None),
            P(("role", "grp", "dev"), None, None, None),
            P(("role", "grp", "dev"), None, None, None),
            P(("role", "grp", "dev")),
            P(("role", "grp", "dev"), None),
            P(("grp", "dev"), None, "role"),
            P(("grp", "dev"), None, "role"),
            P(("grp", "dev"), "role", None),
        ),
        out_specs=P(("role", "grp", "dev"), None),
        check_vma=False,
    )
```

```python
import functools

import jax
import jax.numpy as jnp
from jax import lax
from jax.experimental import pallas as pl
from jax.experimental.pallas import tpu as pltpu
from jax.sharding import PartitionSpec as P


epsilon = 1e-06
rope_base = 1000000.0
LANES = 128
VMEM = pl.BlockSpec(memory_space=pltpu.VMEM)
ANY = pl.BlockSpec(memory_space=pl.ANY)
F32 = jnp.float32
BF16 = jnp.bfloat16


def call(kernel, outs, specs, args, scratch=(), cost=None, limit=None, kept=True):
    flops, moved = cost or (0, 0)
    place = pltpu.VMEM if kept else jax.ShapeDtypeStruct
    return pl.pallas_call(
        kernel,
        out_shape=[place(shape, dtype) for shape, dtype in outs],
        in_specs=list(specs),
        out_specs=[VMEM] * len(outs),
        scratch_shapes=list(scratch),
        cost_estimate=pl.CostEstimate(flops=flops, bytes_accessed=moved, transcendentals=0),
        compiler_params=pltpu.CompilerParams(vmem_limit_bytes=limit),
    )(*args)


def exchange(pieces, axis, size):
    got = [pieces[0]]
    for step in range(1, size):
        got.append(lax.ppermute(pieces[step], axis, [(i, i ^ step) for i in range(size)]))
    return got


def fetch_kernel(count, *refs):
    sources, targets, sems = refs[:count], refs[count : 2 * count], refs[2 * count]
    copies = [pltpu.make_async_copy(a, b, sems.at[i]) for i, (a, b) in enumerate(zip(sources, targets))]
    for copy in copies:
        copy.start()
    for copy in copies:
        copy.wait()


def fetch(*arrays, held=True):
    moved = sum(a.size * a.dtype.itemsize for a in arrays)
    return call(
        functools.partial(fetch_kernel, len(arrays)),
        [(a.shape, a.dtype) for a in arrays],
        [ANY] * len(arrays),
        [pltpu.with_memory_space_constraint(a, pltpu.HBM) if held else a for a in arrays],
        scratch=[pltpu.SemaphoreType.DMA((len(arrays),))],
        cost=(0, moved),
        limit=1 << 20,
    )


def rms(values, gain):
    mean_square = jnp.mean(values * values, axis=-1, keepdims=True)
    return values * lax.rsqrt(mean_square + epsilon) * gain


def stack(refs):
    return jnp.concatenate([ref[...].astype(F32) for ref in refs], axis=0)


def project_kernel(count, *refs):
    blocks, (gain, w_query, w_keyvalue, ids), outs = refs[:count], refs[count : count + 4], refs[count + 4 :]
    rows = blocks[0].shape[0]
    query_width = w_query.shape[1]
    kv_width = w_keyvalue.shape[1]
    picks = ids.shape[0]
    spread = lax.broadcasted_iota(jnp.int32, (picks, LANES), 0) == lax.broadcasted_iota(jnp.int32, (picks, LANES), 1)
    named = lax.dot_general(
        ids[...].astype(F32).astype(BF16),
        jnp.where(spread, 1.0, 0.0).astype(BF16),
        (((0,), (0,)), ((), ())),
        preferred_element_type=F32,
    )
    lane = lax.broadcasted_iota(jnp.int32, named.shape, 1)
    named = jnp.where(lane < picks, named, -1.0).astype(BF16)
    normed = rms(stack(blocks), gain[...]).astype(BF16)
    queries = jnp.dot(normed, w_query[...], preferred_element_type=F32)
    fresh = jnp.dot(normed, w_keyvalue[...], preferred_element_type=F32)
    for step in range(count):
        own = slice(step * rows, (step + 1) * rows)
        outs[step][:, :query_width] = queries[own].astype(BF16)
        outs[step][:, query_width : query_width + kv_width] = fresh[own].astype(BF16)
        outs[step][:, query_width + kv_width :] = named


def turn(values, gain, cosine, sine):
    values = rms(values, gain)
    return values * cosine + pltpu.roll(values, values.shape[1] // 2, 1) * sine


def attend_cache(message, head, gain, cosine, sine, bias, keys, values, scratch):
    rows, _, _, dim = keys.shape
    group = scratch.shape[0] // rows
    for h in range(group):
        piece = message[:, h * dim : (h + 1) * dim].astype(F32)
        scratch[pl.ds(h, rows, stride=group), :] = turn(piece, gain, cosine, sine)
    query = scratch[...].reshape(rows, group, dim).astype(BF16)
    scores = jnp.einsum("rqd,rkd->rqk", query, keys[:, head], preferred_element_type=F32) * dim ** (-0.5)
    scores = scores + bias[:, None, :]
    top = jnp.max(scores, axis=-1, keepdims=True)
    weights = jnp.exp(scores - top)
    total = jnp.sum(weights, axis=-1, keepdims=True)
    mixed = jnp.einsum("rqk,rkd->rqd", weights.astype(BF16), values[:, head], preferred_element_type=F32)
    return query.astype(F32), top, total, mixed


def attend_kernel(steps, *refs):
    count = len(steps)
    me = lax.axis_index("dev")
    messages = refs[:count]
    gain, cosine, sine, bias, keys, values = refs[count : count + 6]
    outs, scratch = refs[count + 7 : -1], refs[-1]
    for i, step in enumerate(steps):
        found = attend_cache(
            messages[i], me ^ step, gain[...], cosine[...], sine[...], bias[...], keys, values, scratch.at[i]
        )
        for out, value in zip(outs[4 * i : 4 * i + 4], found):
            out[...] = jnp.broadcast_to(value, out.shape)


def mix_kernel(count, done, steps, *refs):
    messages, parts = refs[:count], refs[count : count + 4 * done]
    refs = refs[count + 4 * done :]
    q_gain, k_gain, cosine, sine, bias, keys, values = refs[:7]
    outs = refs[7 : 7 + len(steps)]
    scratch, k_rot, v_new, kv_all = refs[7 + len(steps) :]
    me = lax.axis_index("dev")
    rows, heads, _, dim = keys.shape
    group = scratch.shape[1] // rows
    query_width = group * dim
    kv_width = kv_all.shape[2]
    cos, sin = cosine[...], sine[...]
    last = {
        step: attend_cache(messages[step], me ^ step, q_gain[...], cos, sin, bias[...], keys, values, scratch.at[step])
        for step in steps
        if step >= done
    }
    for step in range(count):
        kv_all[me ^ step] = messages[step][:, query_width : query_width + kv_width].astype(F32)
    for h in range(2 * heads):
        column = h * dim
        piece = kv_all[column // kv_width, :, column % kv_width : column % kv_width + dim]
        if h < heads:
            k_rot[h] = turn(piece, k_gain[...], cos, sin).astype(BF16).astype(F32)
        else:
            v_new[h - heads] = piece
    for out, step in reversed(list(zip(outs, steps))):
        head = me ^ step
        if step < done:
            query, top, total, mixed = [ref[...] for ref in parts[4 * step : 4 * step + 4]]
            top, total = top[:, :, :1], total[:, :, :1]
        else:
            query, top, total, mixed = last[step]
        new = jnp.sum(query * k_rot[head][:, None, :], axis=-1, keepdims=True) * dim ** (-0.5)
        highest = jnp.maximum(top, new)
        old = jnp.exp(top - highest)
        new = jnp.exp(new - highest)
        share = 1.0 / (total * old + new)
        found = mixed * (old * share) + (new * share) * v_new[head][:, None, :]
        scratch[step] = found.reshape(rows * group, dim)
        for h in range(group):
            out[:, h * dim : (h + 1) * dim] = scratch[step, pl.ds(h, rows, stride=group), :].astype(BF16)


def out_kernel(count, *refs):
    blocks, w_out, outs = refs[:count], refs[count], refs[count + 1 :]
    rows = blocks[0].shape[0]
    partial = jnp.dot(stack(blocks).astype(BF16), w_out[...], preferred_element_type=F32)
    for step in range(count):
        outs[step][...] = partial[step * rows : (step + 1) * rows].astype(outs[step].dtype)


def ready_kernel(count, *refs):
    blocks, (tokens, gain), (hidden, ready) = refs[:count], refs[count : count + 2], refs[count + 2 :]
    total = blocks[0][...]
    for block in blocks[1:]:
        total = total + block[...].astype(F32)
    total = tokens[...].astype(F32) + total
    hidden[...] = total
    ready[...] = rms(total, gain[...]).astype(BF16)


def route_kernel(count, groups, capacity, *refs):
    messages, outs = refs[:count], refs[count:]
    dev, grp = lax.axis_index("dev"), lax.axis_index("grp")
    rows, columns = messages[0].shape
    total = count * rows
    lane = lax.broadcasted_iota(jnp.int32, (total, LANES), 1)
    down = lax.broadcasted_iota(jnp.int32, (total, total), 0)
    across = lax.broadcasted_iota(jnp.int32, (total, total), 1)
    earlier = jnp.where((across < down) & (across // rows == down // rows), 1.0, 0.0).astype(BF16)
    table = jnp.concatenate([m[:, columns - LANES :].astype(F32) for m in messages], axis=0)
    named = jnp.zeros((total, LANES), F32)
    for step in range(groups):
        expert = ((grp ^ step) * count + dev).astype(F32)
        hit = jnp.max(jnp.where(table == expert, 1.0, 0.0), axis=1, keepdims=True)
        named = jnp.where(lane == step, hit, named)
    rank = jnp.dot(earlier, named.astype(BF16), preferred_element_type=F32)
    source = (lax.broadcasted_iota(jnp.int32, (total, LANES), 0) // rows).astype(F32)
    slot = rank + source * capacity
    first = 0
    for out in outs:
        held = out.shape[0]
        stride = out.shape[1] // groups
        place = lax.broadcasted_iota(jnp.int32, out.shape, 1).astype(F32)
        chosen = jnp.zeros(out.shape, F32)
        for step in range(groups):
            at = slot[:held, step : step + 1] - first
            inside = (at >= 0) & (at < stride) & (named[:held, step : step + 1] > 0)
            chosen = jnp.where((place == at + step * stride) & inside, 1.0, chosen)
        out[...] = chosen.astype(BF16)
        first += stride


def pack_kernel(count, *refs):
    blocks, choice, outs = refs[:count], refs[count], refs[count + 2 :]
    stride = outs[0].shape[0]
    packed = lax.dot_general(
        choice[...], stack(blocks).astype(BF16), (((0,), (0,)), ((), ())), preferred_element_type=F32
    )
    for step, out in enumerate(outs):
        out[...] = packed[step * stride : (step + 1) * stride].astype(BF16)


def expert_kernel(groups, *refs):
    blocks, weights, outs = refs[:groups], refs[groups : groups + 6], refs[groups + 6 :]
    stride = outs[0].shape[0]
    inputs = stack(blocks).astype(BF16)
    total = None
    for half in range(2):
        gate, up, down = weights[3 * half : 3 * half + 3]
        gated = jnp.dot(inputs, gate[...], preferred_element_type=F32)
        upper = jnp.dot(inputs, up[...], preferred_element_type=F32)
        active = (gated / (1.0 + jnp.exp(-gated)) * upper).astype(BF16)
        part = jnp.dot(active, down[...], preferred_element_type=F32)
        total = part if total is None else total + part
    for step, out in enumerate(outs):
        out[...] = total[step * stride : (step + 1) * stride].astype(BF16)


def combine_kernel(groups, sets, start, *refs):
    choices, outs = refs[sets * groups : sets * (groups + 1)], refs[sets * (groups + 1) + 1 :]
    rows = outs[0].shape[0]
    summed = None
    for i, choice in enumerate(choices):
        part = jnp.dot(
            choice[start : start + len(outs) * rows],
            stack(refs[i * groups : (i + 1) * groups]).astype(BF16),
            preferred_element_type=F32,
        )
        summed = part if summed is None else summed + part
    for step, out in enumerate(outs):
        out[...] = summed[step * rows : (step + 1) * rows].astype(out.dtype)


def final_kernel(count, picks, *refs):
    blocks, hidden, out = refs[:count], refs[count], refs[count + 1]
    total = blocks[0][...]
    for block in blocks[1:]:
        total = total + block[...].astype(F32)
    out[...] = (hidden[...] + total / picks).astype(BF16)


def body(
    tokens,
    norm_gain,
    q_gain,
    k_gain,
    post_gain,
    w_query,
    w_keyvalue,
    w_out,
    cache_keys,
    cache_values,
    lengths,
    expert_ids,
    w_gate,
    w_up,
    w_down,
):
    count, groups = lax.axis_size("dev"), lax.axis_size("grp")
    rows, width = tokens.shape
    picks = expert_ids.shape[1]
    heads, places, dim = cache_keys.shape[1:]
    query_width, kv_width = w_query.shape[1], w_keyvalue.shape[1]
    group = query_width // dim
    experts = count * groups
    capacity = min(rows, max(3, (rows * picks + experts - 1) // experts + 1))
    strides = [max(8, count // 2 * capacity // 8 * 8)]
    strides.append(max(8, -(-(count * capacity - strides[0]) // 8) * 8))

    half = count // 2
    near, far = list(range(half)), list(range(half, count))
    swap = [(0, 1), (1, 0)]
    own_weights = [w_gate[0], w_up[0], w_down[0]]
    gathered = exchange([tokens] * count, "dev", count)
    other_weights = [lax.ppermute(w, "role", swap) for w in own_weights]
    query_kept, kv_kept, tokens_kept, gain_kept = fetch(w_query, w_keyvalue, tokens, norm_gain.reshape(1, -1))
    gathered[0] = tokens_kept

    chunks = [near] + [[step] for step in far]
    messages = [None] * count
    for chunk in [near, far]:
        made = call(
            functools.partial(project_kernel, len(chunk)),
            [((rows, query_width + kv_width + LANES), BF16)] * len(chunk),
            [VMEM] * (len(chunk) + 4),
            [*[gathered[step] for step in chunk], gain_kept, query_kept, kv_kept, expert_ids.T],
            cost=(2 * len(chunk) * rows * width * (query_width + kv_width), 3 << 20),
            limit=4 << 20,
        )
        if chunk == near:
            lengths, made = lax.optimization_barrier((lengths, made))
        for step, message in zip(chunk, made):
            messages[step] = message
    frequency = rope_base ** (-jnp.arange(dim // 2, dtype=F32) / (dim // 2))
    angles = lengths.astype(F32)[:, None] * frequency[None, :]
    cosine, sine = jnp.cos(angles), jnp.sin(angles)
    cosine = jnp.concatenate([cosine, cosine], axis=1)
    sine = jnp.concatenate([-sine, sine], axis=1)
    visible = jnp.arange(places, dtype=jnp.int32)[None, :] < lengths[:, None]
    bias = jnp.where(visible, 0.0, -jnp.inf).astype(F32)
    messages = exchange(messages, "dev", count)
    parts = []
    gains = [q_gain.reshape(1, -1), k_gain.reshape(1, -1)]
    flops = 4 * rows * group * places * dim
    for chunk in chunks[:-1]:
        parts += call(
            functools.partial(attend_kernel, chunk),
            [((rows, group, dim), F32)] * (4 * len(chunk)),
            [VMEM] * (len(chunk) + 6) + [ANY],
            [*[messages[step] for step in chunk], gains[0], cosine, sine, bias]
            + [cache_keys, cache_values, parts[-1] if parts else bias],
            scratch=[pltpu.VMEM((len(chunk), rows * group, dim), F32)],
            cost=(len(chunk) * flops, 2 << 20),
            limit=4 << 20,
        )
    mixtures = [None] * count
    for steps in ([1], [0, *range(2, count)]):
        made = call(
            functools.partial(mix_kernel, count, count - 1, steps),
            [((rows, query_width), BF16)] * len(steps),
            [VMEM] * (count + 4 * (count - 1) + 7),
            [*messages, *parts, *gains, cosine, sine, bias, cache_keys, cache_values],
            scratch=[
                pltpu.VMEM((count, rows * group, dim), F32),
                pltpu.VMEM((heads, rows, dim), F32),
                pltpu.VMEM((heads, rows, dim), F32),
                pltpu.VMEM((count, rows, kv_width), F32),
            ],
            cost=(flops, 2 << 20),
            limit=4 << 20,
        )
        for step, mixture in zip(steps, made):
            mixtures[step] = mixture
    choices = call(
        functools.partial(route_kernel, count, groups, capacity),
        [((half * rows, groups * strides[0]), BF16), ((count * rows, groups * strides[1]), BF16)],
        [VMEM] * count,
        [*messages],
        cost=(0, 2 << 20),
        limit=2 << 20,
    )
    mixtures = exchange(mixtures, "dev", count)
    partials = [None] * count
    for chunk in chunks:
        made = call(
            functools.partial(out_kernel, len(chunk)),
            [((rows, width), BF16 if step else F32) for step in chunk],
            [VMEM] * (len(chunk) + 1),
            [*[mixtures[step] for step in chunk], w_out],
            cost=(2 * len(chunk) * rows * width * query_width, 2 << 20),
            limit=4 << 20,
        )
        for step, partial in zip(chunk, made):
            partials[step] = partial
    partials = exchange(partials, "dev", count)
    hidden, ready = call(
        functools.partial(ready_kernel, count),
        [((rows, width), F32), ((rows, width), BF16)],
        [VMEM] * (count + 2),
        [*partials, tokens_kept, post_gain.reshape(1, -1)],
        cost=(0, 1 << 20),
        limit=8 << 20,
    )
    ready = exchange([ready] * count, "dev", count)
    results = []
    after = hidden
    for part, choice, stride in zip((near, near + far), choices, strides):
        packed = call(
            functools.partial(pack_kernel, len(part)),
            [((stride, width), BF16)] * groups,
            [VMEM] * (len(part) + 1) + [ANY],
            [*[ready[step] for step in part], choice, after],
            cost=(0, 1 << 20),
            limit=4 << 20,
        )
        after = packed[0]
        packed = exchange(packed, "grp", groups)
        results.append(
            call(
                functools.partial(expert_kernel, groups),
                [((stride, width), BF16)] * groups,
                [VMEM] * (groups + 6),
                [*packed, *own_weights, *other_weights],
                cost=(6 * groups * stride * width * w_gate.shape[2] * 2, 4 << 20),
                limit=8 << 20,
            )
        )
    sums = [None] * count
    after = hidden
    held = [None, exchange(results[1], "grp", groups)]
    held[0] = exchange(results[0], "grp", groups)
    for part, used in ((far, [1]), (near, [0, 1])):
        made = call(
            functools.partial(combine_kernel, groups, len(used), part[0] * rows),
            [((rows, width), BF16 if step else F32) for step in part],
            [VMEM] * (len(used) * (groups + 1)) + [ANY],
            [*sum([held[i] for i in used], []), *[choices[i] for i in used], after],
            cost=(0, 1 << 20),
            limit=4 << 20,
        )
        after = made[0]
        for step, total in zip(part, made):
            sums[step] = total
    sums = exchange(sums, "dev", count)
    [output] = call(
        functools.partial(final_kernel, count, picks),
        [((rows, width), BF16)],
        [VMEM] * (count + 1),
        [*sums, hidden],
        cost=(0, 1 << 20),
        limit=8 << 20,
        kept=False,
    )
    return output


def rms_scale(values, gain):
    widened = values.astype(jnp.float32)
    mean_square = jnp.mean(widened * widened, axis=-1, keepdims=True)
    return widened * lax.rsqrt(mean_square + epsilon) * gain


def rotate(values, positions):
    half_dim = values.shape[-1] // 2
    frequency = rope_base ** (-jnp.arange(half_dim, dtype=jnp.float32) / half_dim)
    angles = positions.astype(jnp.float32)[:, None, None] * frequency[None, None, :]
    cosine = jnp.cos(angles)
    sine_part = jnp.sin(angles)
    first_half = values[..., :half_dim]
    second_half = values[..., half_dim:]
    return jnp.concatenate(
        [
            first_half * cosine - second_half * sine_part,
            second_half * cosine + first_half * sine_part,
        ],
        axis=-1,
    )


def attend(queries, fresh_kv, cache_keys, cache_values, lengths, q_gain, k_gain):
    batch_rows = queries.shape[0]
    kv_heads = cache_keys.shape[1]
    cache_len = cache_keys.shape[2]
    head_dim = cache_keys.shape[3]
    head_count = queries.shape[1] // head_dim
    group_size = head_count // kv_heads
    scaled_q = rotate(
        rms_scale(queries.reshape(batch_rows, head_count, head_dim), q_gain), lengths
    ).astype(jnp.bfloat16)
    fresh_keys = fresh_kv[:, : kv_heads * head_dim].reshape(batch_rows, kv_heads, head_dim)
    fresh_values = fresh_kv[:, kv_heads * head_dim :].reshape(batch_rows, kv_heads, head_dim)
    scaled_k = rotate(rms_scale(fresh_keys, k_gain), lengths).astype(jnp.bfloat16)
    grouped = scaled_q.reshape(batch_rows, kv_heads, group_size, head_dim)
    factor = head_dim ** (-0.5)
    old_scores = (
        jnp.einsum("rgqd,rgkd->rgqk", grouped, cache_keys, preferred_element_type=jnp.float32)
        * factor
    )
    new_scores = (
        jnp.einsum("rgqd,rgd->rgq", grouped, scaled_k, preferred_element_type=jnp.float32) * factor
    )
    visible = jnp.arange(cache_len, dtype=jnp.int32)[None, :] < lengths[:, None]
    old_scores = jnp.where(visible[:, None, None, :], old_scores, -jnp.inf)
    highest = jnp.maximum(jnp.max(old_scores, axis=-1), new_scores)
    old_weights = jnp.exp(old_scores - highest[..., None])
    new_weights = jnp.exp(new_scores - highest)
    denominator = jnp.sum(old_weights, axis=-1) + new_weights
    old_weights = (old_weights / denominator[..., None]).astype(jnp.bfloat16)
    new_weights = (new_weights / denominator).astype(jnp.bfloat16)
    mixture = jnp.einsum(
        "rgqk,rgkd->rgqd", old_weights, cache_values, preferred_element_type=jnp.float32
    )
    mixture = (
        mixture
        + new_weights.astype(jnp.float32)[..., None]
        * fresh_values.astype(jnp.float32)[:, :, None, :]
    )
    return mixture.reshape(batch_rows, head_count * head_dim).astype(jnp.bfloat16)


def expert_rows(inputs, gate_w, up_w, down_w):
    gate_part = jnp.dot(inputs, gate_w, preferred_element_type=jnp.float32)
    upper_part = jnp.dot(inputs, up_w, preferred_element_type=jnp.float32)
    activated = (jax.nn.silu(gate_part) * upper_part).astype(jnp.bfloat16)
    return jnp.dot(activated, down_w, preferred_element_type=jnp.float32)


def general_body(
    tokens,
    norm_gain,
    q_gain,
    k_gain,
    post_gain,
    w_query,
    w_keyvalue,
    w_out,
    cache_keys,
    cache_values,
    lengths,
    expert_ids,
    w_gate,
    w_up,
    w_down,
):
    normed = rms_scale(tokens, norm_gain).astype(jnp.bfloat16)
    query_width = w_query.shape[1]
    piece = lax.all_gather(normed, "dev", axis=0, tiled=True)
    joined = jnp.concatenate(
        [
            jnp.dot(piece, w_query, preferred_element_type=jnp.float32),
            jnp.dot(piece, w_keyvalue, preferred_element_type=jnp.float32),
        ],
        axis=1,
    )
    projected = joined.astype(jnp.bfloat16)
    queries, fresh_kv = (
        lax.all_to_all(projected[:, :query_width], "dev", split_axis=0, concat_axis=1, tiled=True),
        lax.all_to_all(projected[:, query_width:], "dev", split_axis=0, concat_axis=1, tiled=True),
    )
    mixture = attend(queries, fresh_kv, cache_keys, cache_values, lengths, q_gain, k_gain)
    head_rows = lax.all_to_all(mixture, "dev", split_axis=1, concat_axis=0, tiled=True)
    own_rows = tokens.shape[0]
    attended = lax.psum_scatter(
        jnp.dot(head_rows, w_out, preferred_element_type=jnp.float32).astype(jnp.bfloat16),
        "dev",
        scatter_dimension=0,
        tiled=True,
    ).astype(jnp.float32)
    hidden = tokens.astype(jnp.float32) + attended
    ready = rms_scale(hidden, post_gain).astype(jnp.bfloat16)
    picks = expert_ids.shape[1]
    group_count = lax.axis_size("grp")
    member_count = lax.axis_size("dev")
    expert_count = group_count * member_count
    capacity = min(own_rows, max(3, (own_rows * picks + expert_count - 1) // expert_count + 1))
    model_width = tokens.shape[1]
    flat_ids = expert_ids.reshape(own_rows * picks)
    order_index = jnp.arange(own_rows * picks, dtype=jnp.int32)
    earlier = (flat_ids[:, None] == flat_ids[None, :]) & (
        order_index[None, :] < order_index[:, None]
    )
    slot_index = jnp.sum(earlier.astype(jnp.int32), axis=1)
    position = (flat_ids * capacity + slot_index).reshape(own_rows, picks)
    buffer_rows = jnp.arange(expert_count * capacity, dtype=jnp.int32)
    placing = jnp.any(position[None, :, :] == buffer_rows[:, None, None], axis=2).astype(
        jnp.bfloat16
    )
    outgoing = jnp.dot(placing, ready, preferred_element_type=jnp.float32).astype(jnp.bfloat16)
    arrived = lax.all_to_all(
        outgoing.reshape(expert_count, capacity, model_width),
        ("grp", "dev"),
        split_axis=0,
        concat_axis=0,
        tiled=True,
    )
    arrived = arrived.reshape(expert_count * capacity, model_width)
    full_gate, full_up, full_down = (
        lax.all_gather(w_gate, "role", axis=2, tiled=True),
        lax.all_gather(w_up, "role", axis=2, tiled=True),
        lax.all_gather(w_down, "role", axis=1, tiled=True),
    )
    expert_out = expert_rows(arrived, full_gate[0], full_up[0], full_down[0]).astype(jnp.bfloat16)
    returned = lax.all_to_all(
        expert_out.reshape(expert_count, capacity, model_width),
        ("grp", "dev"),
        split_axis=0,
        concat_axis=0,
        tiled=True,
    )
    returned = returned.reshape(expert_count * capacity, model_width)
    selected = (
        jnp.take(returned, position.reshape(own_rows * picks), axis=0)
        .astype(jnp.float32)
        .reshape(own_rows, picks, model_width)
    )
    output = hidden + jnp.sum(selected, axis=1) / picks
    return output.astype(jnp.bfloat16)


def solution(mesh):
    sizes = dict(mesh.shape)

    def step(*args):
        heads = args[8].shape[1]
        powers = all(sizes[axis] & (sizes[axis] - 1) == 0 for axis in ("grp", "dev"))
        fitted = sizes["dev"] == heads and sizes["role"] == 2 and powers
        if not fitted:
            return general_body(*args)
        return body(*args)

    return jax.shard_map(
        step,
        mesh=mesh,
        in_specs=(
            P(("role", "grp", "dev"), None),
            P(),
            P(),
            P(),
            P(),
            P(None, "dev"),
            P(None, "dev"),
            P("dev", None),
            P(("role", "grp", "dev"), None, None, None),
            P(("role", "grp", "dev"), None, None, None),
            P(("role", "grp", "dev")),
            P(("role", "grp", "dev"), None),
            P(("grp", "dev"), None, "role"),
            P(("grp", "dev"), None, "role"),
            P(("grp", "dev"), "role", None),
        ),
        out_specs=P(("role", "grp", "dev"), None),
        check_vma=False,
    )
```
